256 devices in a mesh: seg: 8 (over x, y_hi), gx: 2 (over y_lo), gz: 16 (over z, core).
Axes of the slice: x: 4, y: 4 (y_hi: 2, y_lo: 2; y = y_hi * 2 + y_lo), z: 8, core: 2. Of those that a mesh axis runs over, the one named last changes fastest.
Arguments:
- terminal: float32 [8, 3, 128, 256, 256], P('seg', None, 'gx', 'gz'), may hold values from -6 to 6
- jump: float32 [8, 3, 128, 256, 256], P('seg', None, 'gx', 'gz'), may hold values from -61 to 61
- tangent: float32 [8, 3, 128, 256, 256], P('seg', None, 'gx', 'gz'), may hold values from -36 to 36
- base_velocity: float32 [256], replicated, may hold values from 0.5 to 2
- base_shear: float32 [256], replicated, may hold values from -2 to 2
Outputs:
- adjoint_field: float32 [8, 3, 128, 256, 256], P('seg', None, 'gx', 'gz')
The draws below stay inside these ranges and needn't reach their ends.
All inputs are finite; a program needn't handle non-finite values. Where the reference program divides by a largest or mean magnitude, that divisor is 1e-20 or more.
Results may differ from the reference program's by a relative error of at most 0.00018.
Values sent between devices are 32-bit elements; how exact they have to be, the bound alone decides.
A program may use at most 64 MiB of HBM per device.

```python
import math
import jax
import jax.numpy as jnp
import numpy as np
from jax import lax

NY = 256
CX = 64
CZ = 16
STEPS = 4
SEG = 8
NX = 128
NZ = 256


def tangent_shape(key):
    base_key = jax.random.fold_in(key, 11)
    noise_key, xscale_key, yscale_key = jax.random.split(base_key, 3)
    full_shape = (SEG, 3, NX, NZ, NY)
    noise = jax.random.truncated_normal(noise_key, -4.0, 4.0, full_shape, jnp.float32)
    xscale = jnp.exp(jax.random.uniform(xscale_key, (SEG, 1, NX, 1, 1), jnp.float32, math.log(0.3), math.log(3.0)))
    yscale = jnp.exp(jax.random.uniform(yscale_key, (SEG, 1, 1, 1, NY), jnp.float32, math.log(0.3), math.log(3.0)))
    zramp = 1.0 + 2.0 * jnp.arange(NZ, dtype=jnp.float32).reshape(1, 1, 1, NZ, 1) / NZ
    return noise * xscale * yscale * zramp / 3.0


def draw_tangent(key, part):
    return tangent_shape(key)


def block_factor(key):
    factor_key = jax.random.fold_in(key, 13)
    base_key, block_key = jax.random.split(factor_key, 2)
    x_blocks = NX // CX
    z_blocks = NZ // CZ
    segment_base = jax.random.uniform(base_key, (SEG, 1, 1, 1, 1, 1, 1), jnp.float32, -1.0, 1.0)
    block_part = jax.random.uniform(block_key, (SEG, 1, x_blocks, 1, z_blocks, 1, 1), jnp.float32, -0.6, 0.6)
    factor = jnp.broadcast_to(segment_base + block_part, (SEG, 1, x_blocks, CX, z_blocks, CZ, 1))
    return factor.reshape(SEG, 1, NX, NZ, 1)


def draw_jump(key, part):
    own_key = jax.random.fold_in(key, 12)
    noise = jax.random.truncated_normal(own_key, -4.0, 4.0, (SEG, 3, NX, NZ, NY), jnp.float32)
    return 0.8 * noise + block_factor(key) * tangent_shape(key)


def shard_levels(key, shape, shards, least, largest):
    def one(dim, shards_of):
        draws = jax.random.uniform(jax.random.fold_in(jax.random.fold_in(key, 6), dim), (shards_of,), jnp.float32, least / len(shards), largest / len(shards))
        return jnp.repeat(jnp.exp(draws), shape[dim] // shards_of).reshape((-1,) + (1,) * (len(shape) - dim - 1))

    level = one(*shards[0])
    for cut in shards[1:]:
        level = level * one(*cut)
    return level


def normal_values(key, extent, scale, reach, cuts=(), held_as=jnp.bfloat16):
    entries = jax.random.normal(key, extent, jnp.float32) * scale
    if len(cuts) > 0:
        entries = shard_levels(key, extent, cuts, -0.22, 0.18) * entries
    return jnp.clip(entries, min=-reach, max=reach).astype(held_as)


def setup_inputs(seed: int = 0) -> dict:
    seeds = jax.random.split(jax.random.key(seed), 6)
    terminal = normal_values(seeds[0], (SEG, 3, NX, NZ, NY), 1.0, 6.0, ((0, 8), (2, 2), (3, 16)), jnp.float32)
    jump = draw_jump(jax.random.fold_in(seeds[5], 71), 0)
    tangent = draw_tangent(jax.random.fold_in(seeds[5], 71), 0)
    base_velocity = jnp.clip(jax.random.uniform(seeds[3], (NY,), jnp.float32, 0.5, 2.0), 0.5, 2.0)
    base_shear = jnp.clip(jax.random.uniform(seeds[4], (NY,), jnp.float32, -2.0, 2.0), -2.0, 2.0)
    return dict(terminal=terminal, jump=jump, tangent=tangent, base_velocity=base_velocity, base_shear=base_shear)


TIME_STEP = 0.15
DIFFUSE = 0.1
WALL_COEF = 2e-4
EPSILON = 1e-6
NEWTON_TURNS = 100


def invert_newton(matrix):
    order = matrix.shape[0]
    identity = np.eye(order)
    scale_one = np.max(np.sum(np.abs(matrix), axis=0))
    scale_inf = np.max(np.sum(np.abs(matrix), axis=1))
    approx = matrix.T / (scale_one * scale_inf)
    for turn_index in range(NEWTON_TURNS):
        approx = approx @ (2.0 * identity - matrix @ approx)
    return approx


def wall_table(points):
    intervals = points - 1
    cheb_nodes = np.cos(np.pi * np.arange(points) / intervals)
    weights = np.ones(points)
    weights[0] = 2.0
    weights[-1] = 2.0
    weights = weights * (-1.0) ** np.arange(points)
    spread = cheb_nodes[:, None] - cheb_nodes[None, :]
    first_deriv = (weights[:, None] / weights[None, :]) / (spread + np.eye(points))
    first_deriv = first_deriv - np.eye(points) * first_deriv.sum(axis=1)[:, None]
    second = first_deriv @ first_deriv
    interior = np.eye(points - 2) - WALL_COEF * second[1:-1, 1:-1]
    helm_table = np.zeros((points, points))
    helm_table[1:-1, 1:-1] = invert_newton(interior)
    return jnp.asarray(helm_table.T, dtype=jnp.float32)


def advance(padded, velocity, shear, table_t):
    center = padded[:, 2:-2, 2:-2, :]
    fwd2_x = padded[:, 4:, 2:-2, :]
    fwd1_x = padded[:, 3:-1, 2:-2, :]
    back1_x = padded[:, 1:-3, 2:-2, :]
    back2_x = padded[:, :-4, 2:-2, :]
    fwd2_z = padded[:, 2:-2, 4:, :]
    fwd1_z = padded[:, 2:-2, 3:-1, :]
    back1_z = padded[:, 2:-2, 1:-3, :]
    back2_z = padded[:, 2:-2, :-4, :]
    advect = (back2_x - fwd2_x + 8.0 * (fwd1_x - back1_x)) / 12.0
    lap_x = (16.0 * (fwd1_x + back1_x) - (fwd2_x + back2_x) - 30.0 * center) / 12.0
    lap_z = (16.0 * (fwd1_z + back1_z) - (fwd2_z + back2_z) - 30.0 * center) / 12.0
    explicit = center + TIME_STEP * velocity * advect + DIFFUSE * (lap_x + lap_z)
    explicit = jnp.concatenate([explicit[:1], explicit[1:2] - TIME_STEP * shear * center[:1], explicit[2:]], axis=0)
    flattened = explicit.reshape(-1, explicit.shape[-1])
    updated = jnp.dot(flattened, table_t, precision=lax.Precision.HIGHEST, preferred_element_type=jnp.float32)
    return updated.reshape(explicit.shape)


def reference(terminal, jump, tangent, base_velocity, base_shear):
    table_t = wall_table(NY)
    received = jnp.roll(terminal, -1, axis=0)

    def segment(segment_items):
        incoming, forcing, direction = segment_items
        started = incoming + forcing
        along_coef = jnp.sum(started * direction) / (jnp.sum(direction * direction) + EPSILON)
        adjoint = started - along_coef * direction
        for step_index in range(STEPS):
            padded = jnp.pad(adjoint, ((0, 0), (2, 2), (2, 2), (0, 0)), mode="wrap")
            adjoint = advance(padded, base_velocity, base_shear, table_t)
        return adjoint

    return lax.map(segment, (received, jump, tangent))
```

```python
import functools

import jax
import jax.numpy as jnp
import ml_dtypes
import numpy as np
from jax import lax
from jax.experimental import pallas as pl
from jax.experimental.pallas import tpu as pltpu
from jax.sharding import PartitionSpec as P

TIME_STEP = 0.15
DIFFUSE = 0.1
WALL_COEF = 0.0002
EPSILON = 1e-06
NEWTON_TURNS = 100
MESH = pl.DeviceIdType.MESH

NCOMP = 3
CX = 64
CZ = 16
LANES = 128
HALO = 8
XB = 16
NXO = CX + 2 * HALO
NXB = NXO + 4
ZIN = 40
ZBUF = 32
ZOUT = (32, 24, 24, 16)
CHUNK = 8
NCH = CX // CHUNK


def invert_newton(matrix):
    order = matrix.shape[0]
    identity = np.eye(order)
    scale_one = np.max(np.sum(np.abs(matrix), axis=0))
    scale_inf = np.max(np.sum(np.abs(matrix), axis=1))
    approx = matrix.T / (scale_one * scale_inf)
    for turn_index in range(NEWTON_TURNS):
        approx = approx @ (2.0 * identity - matrix @ approx)
    return approx


def wall_table(points):
    intervals = points - 1
    cheb_nodes = np.cos(np.pi * np.arange(points) / intervals)
    weights = np.ones(points)
    weights[0] = 2.0
    weights[-1] = 2.0
    weights = weights * (-1.0) ** np.arange(points)
    spread = cheb_nodes[:, None] - cheb_nodes[None, :]
    first_deriv = weights[:, None] / weights[None, :] / (spread + np.eye(points))
    first_deriv = first_deriv - np.eye(points) * first_deriv.sum(axis=1)[:, None]
    second = first_deriv @ first_deriv
    interior = np.eye(points - 2) - WALL_COEF * second[1:-1, 1:-1]
    helm_table = np.zeros((points, points))
    helm_table[1:-1, 1:-1] = invert_newton(interior)
    return helm_table.T.astype(np.float32)


def kernel(
    sizes,
    t_hbm, j_hbm, tan_hbm, coef_ref, hhi_ref, hlo_ref,
    out_hbm,
    tb, b0, w1, w2, w3, res, osend, orecv, ehi, elo, acc, ar_send, ar_recv_a, ar_mid, ar_recv_b,
    load_sem, t_send, t_recv, zs_send, zs_recv, zt_send, zt_recv,
    ra_send, ra_recv, rb_send, rb_recv, o_send, o_recv, out_sem,
):
    nseg, ngx, ngz = sizes
    seg, gx, gz = lax.axis_index("seg"), lax.axis_index("gx"), lax.axis_index("gz")
    nz = ngz // 2
    zc, core = gz // 2, lax.rem(gz, 2)
    before, after = lax.rem(seg + nseg - 1, nseg), lax.rem(seg + 1, nseg)
    zl, zr = lax.rem(gz + ngz - 1, ngz), lax.rem(gz + 1, ngz)
    ogx, ogz = 1 - gx, zc * 2 + (1 - core)
    left, right, partner = (seg, gx, zl), (seg, gx, zr), (seg, ogx, gz)
    group_a = [(seg, gx, ogz), (seg, ogx, gz), (seg, ogx, ogz)]
    group_b = [(seg, gx, lax.rem(zc + o, nz) * 2 + core) for o in range(1, nz)]
    outer = (seg, gx, lax.rem(gz + jnp.where(core == 0, ngz - 1, 1), ngz))

    def loads(start):
        for a, src in ((0, tan_hbm), (1, j_hbm)):
            for c in range(NCOMP):
                for h in range(2):
                    cp = pltpu.make_async_copy(
                        src.at[0, c, :, :, pl.ds(h * LANES, LANES)],
                        b0.at[a * NCOMP + c, h, pl.ds(2 + HALO, CX), pl.ds(HALO, CZ), :],
                        load_sem.at[(a * NCOMP + c) * 2 + h],
                    )
                    if start:
                        cp.start()
                    else:
                        cp.wait()

    loads(True)

    barrier = pltpu.get_barrier_semaphore()
    peers = [(before, gx, gz), (after, gx, gz), outer] + group_a + group_b
    for d in peers:
        pl.semaphore_signal(barrier, inc=1, device_id=d, device_id_type=MESH)
    pl.semaphore_wait(barrier, len(peers))

    def t_copy(c, i):
        rows = pl.ds(i * CHUNK, CHUNK)
        return pltpu.make_async_remote_copy(
            src_ref=t_hbm.at[0, c, rows],
            dst_ref=tb.at[c, rows],
            send_sem=t_send.at[c * NCH + i],
            recv_sem=t_recv.at[c * NCH + i],
            device_id=(before, gx, gz),
            device_id_type=MESH,
        )

    for c in range(NCOMP):
        @pl.loop(0, NCH)
        def _(i):
            t_copy(c, i).start()

    def zero_pads(s, _):
        for h in range(2):
            for lo, hi in ((0, 2 + HALO), (2 + HALO + CX, NXB)):
                b0[s, h, lo:hi, :, :] = jnp.zeros((hi - lo, ZIN, LANES), jnp.float32)
            b0[s, h, 2 + HALO:2 + HALO + CX, 2 * HALO + CZ:, :] = jnp.zeros(
                (CX, ZIN - 2 * HALO - CZ, LANES), jnp.float32)
        return 0

    lax.fori_loop(0, 2 * NCOMP, zero_pads, 0)
    for w in (w1, w2, w3):
        for s in range(2):
            for h in range(2):
                for lo in (0, NXB - 2):
                    w[s, h, lo:lo + 2, :, :] = jnp.zeros((2, ZBUF, LANES), jnp.float32)
                w[s, h, 2:NXB - 2, 24:, :] = jnp.zeros((NXB - 4, 8, LANES), jnp.float32)
    acc[...] = jnp.zeros_like(acc)

    def strip(slot, x0, nx, side, send_sem, recv_sem):
        rows = pl.ds(2 + HALO + x0, nx)
        src = pl.ds(HALO, HALO) if side == 0 else pl.ds(HALO + CZ - HALO, HALO)
        dst = pl.ds(HALO + CZ, HALO) if side == 0 else pl.ds(0, HALO)
        return pltpu.make_async_remote_copy(
            src_ref=b0.at[slot, :, rows, src, :],
            dst_ref=b0.at[slot, :, rows, dst, :],
            send_sem=send_sem,
            recv_sem=recv_sem,
            device_id=left if side == 0 else right,
            device_id_type=MESH,
        )

    def tan_strip(c, side):
        k = c * 2 + side
        return strip(c, 0, CX, side, zs_send.at[k], zs_recv.at[k])

    def start_strip(c, i, side):
        k = (c * NCH + i) * 2 + side
        return strip(NCOMP + c, i * CHUNK, CHUNK, side, zt_send.at[k], zt_recv.at[k])

    loads(False)
    for c in range(NCOMP):
        for side in range(2):
            tan_strip(c, side).start()

    def dot_rows(first, second):
        prod = first * second
        return jnp.sum(prod.reshape(-1, 8, LANES), axis=0)

    def square(i, _):
        c, x = i // NCH, lax.rem(i, NCH) * CHUNK
        for h in range(2):
            tau = b0[c, h, pl.ds(2 + HALO + x, CHUNK), HALO:HALO + CZ, :]
            acc[1] += dot_rows(tau, tau)
        return 0

    lax.fori_loop(0, NCOMP * NCH, square, 0)

    def arrive(c):
        def piece(i, _):
            t_copy(c, i).wait_recv()
            rows = pl.ds(2 + HALO + i * CHUNK, CHUNK)
            for h in range(2):
                started = b0[NCOMP + c, h, rows, HALO:HALO + CZ, :] + tb[
                    c, pl.ds(i * CHUNK, CHUNK), :, h * LANES:(h + 1) * LANES]
                b0[NCOMP + c, h, rows, HALO:HALO + CZ, :] = started
                acc[0] += dot_rows(started, b0[c, h, rows, HALO:HALO + CZ, :])
            start_strip(c, i, 0).start()
            start_strip(c, i, 1).start()
            return 0

        lax.fori_loop(0, NCH, piece, 0)

    def reduce_a(o):
        return pltpu.make_async_remote_copy(
            src_ref=ar_send, dst_ref=ar_recv_a.at[o], send_sem=ra_send.at[o], recv_sem=ra_recv.at[o],
            device_id=group_a[o], device_id_type=MESH)

    def reduce_b(o):
        return pltpu.make_async_remote_copy(
            src_ref=ar_mid, dst_ref=ar_recv_b.at[o], send_sem=rb_send.at[o], recv_sem=rb_recv.at[o],
            device_id=group_b[o], device_id_type=MESH)

    def outflow(c):
        return pltpu.make_async_remote_copy(
            src_ref=osend.at[c], dst_ref=orecv.at[c], send_sem=o_send.at[c], recv_sem=o_recv.at[c],
            device_id=partner, device_id_type=MESH)

    def reduce_all():
        row = lax.broadcasted_iota(jnp.int32, (8, LANES), 0)
        top = jnp.sum(acc[0], axis=0, keepdims=True)
        low = jnp.sum(acc[1], axis=0, keepdims=True)
        ar_send[...] = jnp.where(row == 0, top, jnp.where(row == 1, low, 0.0))
        for o in range(3):
            reduce_a(o).start()
        for o in range(3):
            reduce_a(o).wait_recv()
        ar_mid[...] = ar_send[...] + ar_recv_a[0] + (ar_recv_a[1] + ar_recv_a[2])
        for o in range(nz - 1):
            reduce_b(o).start()
        for o in range(nz - 1):
            reduce_b(o).wait_recv()
        total = ar_mid[...]
        for o in range(nz - 1):
            total += ar_recv_b[o]
        sums = jnp.sum(total, axis=1, keepdims=True)
        acc[0] = jnp.broadcast_to(sums[0:1] / (sums[1:2] + EPSILON), (8, LANES))

    def send_outflow(c):
        along = acc[0, 0:1, 0:1]

        def put(i, _):
            osend[c, 0, i] = res[1, c, HALO + CX + i] - along * res[0, c, HALO + CX + i]
            osend[c, 1, i] = res[1, c, i] - along * res[0, c, i]
            return 0

        lax.fori_loop(0, HALO, put, 0)
        outflow(c).start()

    bufs = (b0, w1, w2, w3)

    def step(k, n, a, c):
        half_set = jnp.minimum(c, 1)
        z = ZOUT[k]
        src = bufs[k]
        slot = n if k == 0 else half_set
        slot0 = a * NCOMP if k == 0 else 0
        sheared = jnp.where(c == 1, 1.0, 0.0).astype(jnp.float32)

        def block(b, _):
            for p in range(XB // 2):
                for h in range(2):
                    cs = [coef_ref[r:r + 1, h * LANES:(h + 1) * LANES] for r in range(5)]
                    shear = cs[4] * sheared
                    both = []
                    for q in range(2):
                        i = b * XB + 2 * p + q

                        def at(dx, dz):
                            return src[slot, h, i + 2 + dx, 2 + dz:2 + dz + z, :]

                        e = 0.5 * at(0, 0)
                        e += (DIFFUSE * 16.0 / 12.0) * (at(0, 1) + at(0, -1))
                        e += (-DIFFUSE / 12.0) * (at(0, 2) + at(0, -2))
                        e += cs[0] * at(1, 0) + cs[1] * at(-1, 0)
                        e += cs[2] * at(2, 0) + cs[3] * at(-2, 0)
                        e += shear * src[slot0, h, i + 2, 2:2 + z, :]
                        both.append(e)
                    e = jnp.concatenate(both, axis=0)
                    hi = e.astype(jnp.bfloat16)
                    lo = (e - hi.astype(jnp.float32)).astype(jnp.bfloat16)
                    ehi[2 * p * z:2 * (p + 1) * z, h * LANES:(h + 1) * LANES] = hi
                    elo[2 * p * z:2 * (p + 1) * z, h * LANES:(h + 1) * LANES] = lo
            m = XB * z
            out = jnp.dot(ehi[:m], hhi_ref[...], preferred_element_type=jnp.float32)
            out += jnp.dot(elo[:m], hhi_ref[...], preferred_element_type=jnp.float32)
            out += jnp.dot(ehi[:m], hlo_ref[...], preferred_element_type=jnp.float32)
            if k < 3:
                dst = bufs[k + 1]
                for h in range(2):
                    dst[half_set, h, pl.ds(2 + b * XB, XB), 0:z, :] = out[
                        :, h * LANES:(h + 1) * LANES].reshape(XB, z, LANES)
            else:
                res[a, c, pl.ds(b * XB, XB)] = out.reshape(XB, z, 2 * LANES)
            return 0

        lax.fori_loop(0, NXO // XB, block, 0)

    def item(n, _):
        a, c = n // NCOMP, lax.rem(n, NCOMP)

        @pl.when(a == 0)
        def _():
            for side in range(2):
                tan_strip(c, side).wait_recv()

        @pl.when(a == 1)
        def _():
            arrive(c)

        @pl.when(n == 2 * NCOMP - 1)
        def _():
            reduce_all()
            for d in range(NCOMP - 1):
                send_outflow(d)

        @pl.when(a == 1)
        def _():
            def strips(i, _):
                start_strip(c, i, 0).wait_recv()
                start_strip(c, i, 1).wait_recv()
                return 0

            lax.fori_loop(0, NCH, strips, 0)

        for k in range(4):
            step(k, n, a, c)
        return 0

    lax.fori_loop(0, 2 * NCOMP, item, 0)
    send_outflow(NCOMP - 1)

    along = acc[0, 0:1, 0:1]

    def write(c, lo, n, k):
        return pltpu.make_async_copy(
            tb.at[c, pl.ds(lo, n)], out_hbm.at[0, c, pl.ds(lo, n)], out_sem.at[c * 3 + k])

    inner = CX - 2 * HALO
    for c in range(NCOMP):
        def mix(i, _):
            tb[c, HALO + i] = res[1, c, 2 * HALO + i] - along * res[0, c, 2 * HALO + i]
            return 0

        lax.fori_loop(0, inner, mix, 0)
        write(c, HALO, inner, 0).start()
    for c in range(NCOMP):
        outflow(c).wait_recv()

        def edges(i, _):
            for side, at in ((0, 0), (1, CX - HALO)):
                own = res[1, c, HALO + at + i] - along * res[0, c, HALO + at + i]
                tb[c, at + i] = own + orecv[c, side, i]
            return 0

        lax.fori_loop(0, HALO, edges, 0)
        write(c, 0, HALO, 1).start()
        write(c, CX - HALO, HALO, 2).start()

    for c in range(NCOMP):
        write(c, HALO, inner, 0).wait()
        write(c, 0, HALO, 1).wait()
        write(c, CX - HALO, HALO, 2).wait()
        outflow(c).wait_send()
        for side in range(2):
            tan_strip(c, side).wait_send()

        @pl.loop(0, NCH)
        def _(i):
            t_copy(c, i).wait_send()
            start_strip(c, i, 0).wait_send()
            start_strip(c, i, 1).wait_send()
    for o in range(3):
        reduce_a(o).wait_send()
    for o in range(nz - 1):
        reduce_b(o).wait_send()


def shards(sizes, terminal, jump, tangent, base_velocity, base_shear):
    table = wall_table(base_velocity.shape[0])
    high = table.astype(ml_dtypes.bfloat16)
    low = (table - high.astype(np.float32)).astype(ml_dtypes.bfloat16)
    near, far = DIFFUSE * 16.0 / 12.0, DIFFUSE / 12.0
    push = TIME_STEP * base_velocity
    coefs = jnp.stack(
        [
            push * (8.0 / 12.0) + near,
            push * (-8.0 / 12.0) + near,
            push * (-1.0 / 12.0) - far,
            push * (1.0 / 12.0) - far,
            -TIME_STEP * base_shear,
        ]
        + [jnp.zeros_like(push)] * 3
    )
    nz = sizes[2] // 2
    f32 = jnp.float32
    dma = pltpu.SemaphoreType.DMA
    hbm = pl.BlockSpec(memory_space=pl.ANY)
    vmem = pl.BlockSpec(memory_space=pltpu.VMEM)
    lanes2 = 2 * LANES
    return pl.pallas_call(
        functools.partial(kernel, sizes),
        out_shape=jax.ShapeDtypeStruct(terminal.shape, f32),
        in_specs=[hbm, hbm, hbm, vmem, vmem, vmem],
        out_specs=hbm,
        scratch_shapes=[
            pltpu.VMEM((NCOMP, CX, CZ, lanes2), f32),
            pltpu.VMEM((2 * NCOMP, 2, NXB, ZIN, LANES), f32),
            pltpu.VMEM((2, 2, NXB, ZBUF, LANES), f32),
            pltpu.VMEM((2, 2, NXB, ZBUF, LANES), f32),
            pltpu.VMEM((2, 2, NXB, ZBUF, LANES), f32),
            pltpu.VMEM((2, NCOMP, NXO, CZ, lanes2), f32),
            pltpu.VMEM((NCOMP, 2, HALO, CZ, lanes2), f32),
            pltpu.VMEM((NCOMP, 2, HALO, CZ, lanes2), f32),
            pltpu.VMEM((XB * ZBUF, lanes2), jnp.bfloat16),
            pltpu.VMEM((XB * ZBUF, lanes2), jnp.bfloat16),
            pltpu.VMEM((2, 8, LANES), f32),
            pltpu.VMEM((8, LANES), f32),
            pltpu.VMEM((3, 8, LANES), f32),
            pltpu.VMEM((8, LANES), f32),
            pltpu.VMEM((nz - 1, 8, LANES), f32),
            dma((4 * NCOMP,)),
            dma((NCOMP * NCH,)),
            dma((NCOMP * NCH,)),
            dma((NCOMP * 2,)),
            dma((NCOMP * 2,)),
            dma((NCOMP * NCH * 2,)),
            dma((NCOMP * NCH * 2,)),
            dma((3,)),
            dma((3,)),
            dma((nz - 1,)),
            dma((nz - 1,)),
            dma((NCOMP,)),
            dma((NCOMP,)),
            dma((3 * NCOMP,)),
        ],
        compiler_params=pltpu.CompilerParams(
            collective_id=0, has_side_effects=True, vmem_limit_bytes=58 * 1024 * 1024
        ),
    )(terminal, jump, tangent, coefs, jnp.asarray(high), jnp.asarray(low))


def solution(mesh):
    sizes = tuple(mesh.shape[name] for name in ("seg", "gx", "gz"))
    split = P("seg", None, "gx", "gz", None)
    return jax.shard_map(
        functools.partial(shards, sizes),
        mesh=mesh,
        in_specs=(split, split, split, P(), P()),
        out_specs=split,
        check_vma=False,
    )
```

```python
import functools

import jax
import jax.numpy as jnp
import ml_dtypes
import numpy as np
from jax import lax
from jax.experimental import pallas as pl
from jax.experimental.pallas import tpu as pltpu
from jax.sharding import PartitionSpec as P

TIME_STEP = 0.15
DIFFUSE = 0.1
WALL_COEF = 0.0002
EPSILON = 1e-06
NEWTON_TURNS = 100
MESH = pl.DeviceIdType.MESH

NCOMP = 3
CX = 64
CZ = 16
LANES = 128
HALO = 8
XB = 16
NXO = CX + 2 * HALO
NXB = NXO + 4
ZIN = 40
ZBUF = 32
ZOUT = (32, 24, 24, 16)
CHUNK = 8
NCH = CX // CHUNK
AHEAD = 5


def invert_newton(matrix):
    order = matrix.shape[0]
    identity = np.eye(order)
    scale_one = np.max(np.sum(np.abs(matrix), axis=0))
    scale_inf = np.max(np.sum(np.abs(matrix), axis=1))
    approx = matrix.T / (scale_one * scale_inf)
    for turn_index in range(NEWTON_TURNS):
        approx = approx @ (2.0 * identity - matrix @ approx)
    return approx


def wall_table(points):
    intervals = points - 1
    cheb_nodes = np.cos(np.pi * np.arange(points) / intervals)
    weights = np.ones(points)
    weights[0] = 2.0
    weights[-1] = 2.0
    weights = weights * (-1.0) ** np.arange(points)
    spread = cheb_nodes[:, None] - cheb_nodes[None, :]
    first_deriv = weights[:, None] / weights[None, :] / (spread + np.eye(points))
    first_deriv = first_deriv - np.eye(points) * first_deriv.sum(axis=1)[:, None]
    second = first_deriv @ first_deriv
    interior = np.eye(points - 2) - WALL_COEF * second[1:-1, 1:-1]
    helm_table = np.zeros((points, points))
    helm_table[1:-1, 1:-1] = invert_newton(interior)
    return helm_table.T.astype(np.float32)


def kernel(
    sizes,
    t_hbm, j_hbm, tan_hbm, vel_hbm, shear_hbm, hhi_hbm, hlo_hbm,
    out_hbm,
    tb, b0, w1, w2, w3, res, osend, orecv, oraw, ehi, elo, vel_ref, shear_ref, hhi_ref, hlo_ref, coef_ref, acc, ar_send, ar_recv_a, ar_mid, ar_recv_b,
    load_sem, const_sem, t_send, t_recv, zs_send, zs_recv, zt_send, zt_recv,
    ra_send, ra_recv, rb_send, rb_recv, o_send, o_recv, or_send, or_recv, out_sem,
):
    nseg, ngx, ngz = sizes
    seg, gx, gz = lax.axis_index("seg"), lax.axis_index("gx"), lax.axis_index("gz")
    nz = ngz // 2
    zc, core = gz // 2, lax.rem(gz, 2)
    before, after = lax.rem(seg + nseg - 1, nseg), lax.rem(seg + 1, nseg)
    zl, zr = lax.rem(gz + ngz - 1, ngz), lax.rem(gz + 1, ngz)
    ogx, ogz = 1 - gx, zc * 2 + (1 - core)
    left, right, partner = (seg, gx, zl), (seg, gx, zr), (seg, ogx, gz)
    group_a = [(seg, gx, ogz), (seg, ogx, gz), (seg, ogx, ogz)]
    group_b = [(seg, gx, lax.rem(zc + o, nz) * 2 + core) for o in range(1, nz)]
    outer = (seg, gx, lax.rem(gz + jnp.where(core == 0, ngz - 1, 1), ngz))

    def loads(start):
        for i, (src, dst) in enumerate((
            (vel_hbm, vel_ref), (shear_hbm, shear_ref), (hhi_hbm, hhi_ref), (hlo_hbm, hlo_ref),
        )):
            cp = pltpu.make_async_copy(src, dst, const_sem.at[i])
            if start:
                cp.start()
            else:
                cp.wait()
        for a, src in ((0, tan_hbm), (1, j_hbm)):
            for c in range(NCOMP):
                for h in range(2):
                    cp = pltpu.make_async_copy(
                        src.at[0, c, :, :, pl.ds(h * LANES, LANES)],
                        b0.at[a * NCOMP + c, h, pl.ds(2 + HALO, CX), pl.ds(HALO, CZ), :],
                        load_sem.at[(a * NCOMP + c) * 2 + h],
                    )
                    if start:
                        cp.start()
                    else:
                        cp.wait()

    barrier = pltpu.get_barrier_semaphore()
    peers = [(before, gx, gz), (after, gx, gz), outer] + group_a + group_b
    for d in peers:
        pl.semaphore_signal(barrier, inc=1, device_id=d, device_id_type=MESH)
    loads(True)
    pl.semaphore_wait(barrier, len(peers))

    def t_copy(c, i):
        rows = pl.ds(i * CHUNK, CHUNK)
        return pltpu.make_async_remote_copy(
            src_ref=t_hbm.at[0, c, rows],
            dst_ref=tb.at[c, rows],
            send_sem=t_send.at[c * NCH + i],
            recv_sem=t_recv.at[c * NCH + i],
            device_id=(before, gx, gz),
            device_id_type=MESH,
        )

    for i in range(AHEAD):
        t_copy(i // NCH, i % NCH).start()

    def zero_pads(s, _):
        for h in range(2):
            for lo, hi in ((0, 2 + HALO), (2 + HALO + CX, NXB)):
                b0[s, h, lo:hi, :, :] = jnp.zeros((hi - lo, ZIN, LANES), jnp.float32)
            b0[s, h, 2 + HALO:2 + HALO + CX, 2 * HALO + CZ:, :] = jnp.zeros(
                (CX, ZIN - 2 * HALO - CZ, LANES), jnp.float32)
        return 0

    lax.fori_loop(0, 2 * NCOMP, zero_pads, 0)
    for w in (w1, w2, w3):
        for s in range(2):
            for h in range(2):
                for lo in (0, NXB - 2):
                    w[s, h, lo:lo + 2, :, :] = jnp.zeros((2, ZBUF, LANES), jnp.float32)
                w[s, h, 2:NXB - 2, 24:, :] = jnp.zeros((NXB - 4, 8, LANES), jnp.float32)
    acc[...] = jnp.zeros_like(acc)
    def strip(slot, x0, nx, side, send_sem, recv_sem):
        rows = pl.ds(2 + HALO + x0, nx)
        src = pl.ds(HALO, HALO) if side == 0 else pl.ds(HALO + CZ - HALO, HALO)
        dst = pl.ds(HALO + CZ, HALO) if side == 0 else pl.ds(0, HALO)
        return pltpu.make_async_remote_copy(
            src_ref=b0.at[slot, :, rows, src, :],
            dst_ref=b0.at[slot, :, rows, dst, :],
            send_sem=send_sem,
            recv_sem=recv_sem,
            device_id=left if side == 0 else right,
            device_id_type=MESH,
        )

    def tan_strip(c, side):
        k = c * 2 + side
        return strip(c, 0, CX, side, zs_send.at[k], zs_recv.at[k])

    def start_strip(c, i, side):
        k = (c * NCH + i) * 2 + side
        return strip(NCOMP + c, i * CHUNK, CHUNK, side, zt_send.at[k], zt_recv.at[k])

    loads(False)
    near, far = DIFFUSE * 16.0 / 12.0, DIFFUSE / 12.0
    push = TIME_STEP * vel_ref[...]
    coef_ref[0:1, :] = push * (8.0 / 12.0) + near
    coef_ref[1:2, :] = push * (-8.0 / 12.0) + near
    coef_ref[2:3, :] = push * (-1.0 / 12.0) - far
    coef_ref[3:4, :] = push * (1.0 / 12.0) - far
    coef_ref[4:5, :] = -TIME_STEP * shear_ref[...]
    for c in range(NCOMP):
        for side in range(2):
            tan_strip(c, side).start()

    def dot_rows(first, second):
        prod = first * second
        return jnp.sum(prod.reshape(-1, 8, LANES), axis=0)

    def square(i, _):
        c, x = i // NCH, lax.rem(i, NCH) * CHUNK
        for h in range(2):
            tau = b0[c, h, pl.ds(2 + HALO + x, CHUNK), HALO:HALO + CZ, :]
            acc[1] += dot_rows(tau, tau)
        return 0

    lax.fori_loop(0, NCOMP * NCH, square, 0)

    def arrive(c):
        def piece(i, _):
            t_copy(c, i).wait_recv()
            rows = pl.ds(2 + HALO + i * CHUNK, CHUNK)
            for h in range(2):
                started = b0[NCOMP + c, h, rows, HALO:HALO + CZ, :] + tb[
                    c, pl.ds(i * CHUNK, CHUNK), :, h * LANES:(h + 1) * LANES]
                b0[NCOMP + c, h, rows, HALO:HALO + CZ, :] = started
                acc[0] += dot_rows(started, b0[c, h, rows, HALO:HALO + CZ, :])
            start_strip(c, i, 0).start()
            start_strip(c, i, 1).start()
            return 0

        lax.fori_loop(0, NCH, piece, 0)

    def reduce_a(o):
        return pltpu.make_async_remote_copy(
            src_ref=ar_send, dst_ref=ar_recv_a.at[o], send_sem=ra_send.at[o], recv_sem=ra_recv.at[o],
            device_id=group_a[o], device_id_type=MESH)

    def reduce_b(o):
        return pltpu.make_async_remote_copy(
            src_ref=ar_mid, dst_ref=ar_recv_b.at[o], send_sem=rb_send.at[o], recv_sem=rb_recv.at[o],
            device_id=group_b[o], device_id_type=MESH)

    def outflow(c):
        sides = pl.ds(1, 1) if c == 0 else pl.ds(0, 2)
        return pltpu.make_async_remote_copy(
            src_ref=osend.at[c, sides], dst_ref=orecv.at[c, sides],
            send_sem=o_send.at[c], recv_sem=o_recv.at[c],
            device_id=partner, device_id_type=MESH)

    def raw_outflow(a):
        return pltpu.make_async_remote_copy(
            src_ref=res.at[a, 0, pl.ds(HALO + CX, HALO)], dst_ref=oraw.at[a],
            send_sem=or_send.at[a], recv_sem=or_recv.at[a],
            device_id=partner, device_id_type=MESH)

    def reduce_all():
        row = lax.broadcasted_iota(jnp.int32, (8, LANES), 0)
        top = jnp.sum(acc[0], axis=0, keepdims=True)
        low = jnp.sum(acc[1], axis=0, keepdims=True)
        ar_send[...] = jnp.where(row == 0, top, jnp.where(row == 1, low, 0.0))
        for o in range(3):
            reduce_a(o).start()
        for o in range(3):
            reduce_a(o).wait_recv()
        ar_mid[...] = ar_send[...] + ar_recv_a[0] + (ar_recv_a[1] + ar_recv_a[2])
        for o in range(nz - 1):
            reduce_b(o).start()
        for o in range(nz - 1):
            reduce_b(o).wait_recv()
        total = ar_mid[...]
        for o in range(nz - 1):
            total += ar_recv_b[o]
        sums = jnp.sum(total, axis=1, keepdims=True)
        acc[0] = jnp.broadcast_to(sums[0:1] / (sums[1:2] + EPSILON), (8, LANES))

    def send_outflow(c):
        along = acc[0, 0:1, 0:1]

        for side, at in ((0, HALO + CX), (1, 0)):
            if c > 0 or side > 0:
                osend[c, side] = res[1, c, at:at + HALO] - along * res[0, c, at:at + HALO]
        outflow(c).start()

    bufs = (b0, w1, w2, w3)

    def advance(k, n, a, c, first, count, sheared):
        half_set = jnp.minimum(c, 1)
        z = ZOUT[k]
        m = count * z
        src = bufs[k]
        slot = n if k == 0 else half_set
        slot0 = a * NCOMP if k == 0 else 0
        for h in range(2):
            cols = slice(h * LANES, (h + 1) * LANES)
            cs = [coef_ref[r:r + 1, cols] for r in range(5)]
            rows = {}

            def row(i):
                if i not in rows:
                    rows[i] = src[slot, h, first + i, 2:2 + z, :]
                return rows[i]

            for p in range(count // 2):
                both = []
                for i in (2 * p, 2 * p + 1):

                    def at(dz):
                        return src[slot, h, first + i + 2, 2 + dz:2 + dz + z, :]

                    e = 0.5 * row(i + 2)
                    e += (DIFFUSE * 16.0 / 12.0) * (at(1) + at(-1))
                    e += (-DIFFUSE / 12.0) * (at(2) + at(-2))
                    e += cs[0] * row(i + 3) + cs[1] * row(i + 1)
                    e += cs[2] * row(i + 4) + cs[3] * row(i)
                    if sheared:
                        e += cs[4] * src[slot0, h, first + i + 2, 2:2 + z, :]
                    both.append(e)
                e = jnp.concatenate(both, axis=0)
                hi = e.astype(jnp.bfloat16)
                ehi[2 * p * z:2 * (p + 1) * z, cols] = hi
                elo[2 * p * z:2 * (p + 1) * z, cols] = (e - hi.astype(jnp.float32)).astype(jnp.bfloat16)
        high = ehi[:m]
        out = jnp.dot(
            jnp.concatenate([high, elo[:m], high], axis=1),
            jnp.concatenate([hhi_ref[...], hhi_ref[...], hlo_ref[...]], axis=0),
            preferred_element_type=jnp.float32,
        )
        if k < 3:
            for h in range(2):
                bufs[k + 1][half_set, h, pl.ds(2 + first, count), 0:z, :] = out[
                    :, h * LANES:(h + 1) * LANES].reshape(count, z, LANES)
        else:
            res[a, c, pl.ds(first, count)] = out.reshape(count, z, 2 * LANES)

    def steps(n, a, c, sheared):
        for k in range(4):
            def block(b, _):
                advance(k, n, a, c, b * XB, XB, sheared)
                return 0

            lax.fori_loop(0, NXO // XB, block, 0)
            sent = n * 4 + k

            @pl.when(sent < NCOMP * NCH - AHEAD)
            def _():
                t_copy(sent // NCH, lax.rem(sent, NCH)).wait_send()
                later = sent + AHEAD
                t_copy(later // NCH, lax.rem(later, NCH)).start()

    def item(n, _):
        a, c = n // NCOMP, lax.rem(n, NCOMP)

        @pl.when(a == 0)
        def _():
            for side in range(2):
                tan_strip(c, side).wait_recv()

        @pl.when(a == 1)
        def _():
            arrive(c)

        @pl.when(n == 2 * NCOMP - 1)
        def _():
            for d in range(2):
                raw_outflow(d).start()
            reduce_all()
            for d in range(NCOMP - 1):
                send_outflow(d)

        @pl.when(a == 1)
        def _():
            def strips(i, _):
                start_strip(c, i, 0).wait_recv()
                start_strip(c, i, 1).wait_recv()
                return 0

            lax.fori_loop(0, NCH, strips, 0)

        @pl.when(n == 2 * NCOMP - 1)
        def _():
            for k in range(4):
                def edge(e, _):
                    advance(k, n, a, c, HALO - 2 * (k + 1) + e * (CX + 4 * (k + 1) - HALO), HALO, False)
                    return 0

                lax.fori_loop(0, 2, edge, 0)
            send_outflow(NCOMP - 1)

        @pl.when(c == 1)
        def _():
            steps(n, a, c, True)

        @pl.when(c != 1)
        def _():
            steps(n, a, c, False)
        return 0

    lax.fori_loop(0, 2 * NCOMP, item, 0)
    along = acc[0, 0:1, 0:1]

    def write(c, lo, n, k):
        return pltpu.make_async_copy(
            tb.at[c, pl.ds(lo, n)], out_hbm.at[0, c, pl.ds(lo, n)], out_sem.at[c * 3 + k])

    inner = CX - 2 * HALO
    for c in range(NCOMP):
        def mix(i, _):
            rows = pl.ds(2 * HALO + i * HALO, HALO)
            tb[c, pl.ds(HALO + i * HALO, HALO)] = res[1, c, rows] - along * res[0, c, rows]
            return 0

        lax.fori_loop(0, inner // HALO, mix, 0)
        write(c, HALO, inner, 0).start()
    for d in range(2):
        raw_outflow(d).wait_recv()
    for c in range(NCOMP):
        outflow(c).wait_recv()
        for side, at in ((0, 0), (1, CX - HALO)):
            own = res[1, c, HALO + at:2 * HALO + at] - along * res[0, c, HALO + at:2 * HALO + at]
            if c == 0 and side == 0:
                other = oraw[1] - along * oraw[0]
            else:
                other = orecv[c, side]
            tb[c, at:at + HALO] = own + other
        write(c, 0, HALO, 1).start()
        write(c, CX - HALO, HALO, 2).start()

    for c in range(NCOMP):
        write(c, HALO, inner, 0).wait()
        write(c, 0, HALO, 1).wait()
        write(c, CX - HALO, HALO, 2).wait()
        outflow(c).wait_send()
        for side in range(2):
            tan_strip(c, side).wait_send()

        @pl.loop(0, NCH)
        def _(i):
            @pl.when(c * NCH + i >= NCOMP * NCH - AHEAD)
            def _():
                t_copy(c, i).wait_send()

            start_strip(c, i, 0).wait_send()
            start_strip(c, i, 1).wait_send()
    for d in range(2):
        raw_outflow(d).wait_send()
    for o in range(3):
        reduce_a(o).wait_send()
    for o in range(nz - 1):
        reduce_b(o).wait_send()


def shards(sizes, terminal, jump, tangent, base_velocity, base_shear):
    table = wall_table(base_velocity.shape[0])
    high = table.astype(ml_dtypes.bfloat16)
    low = (table - high.astype(np.float32)).astype(ml_dtypes.bfloat16)
    nz = sizes[2] // 2
    f32 = jnp.float32
    dma = pltpu.SemaphoreType.DMA
    hbm = pl.BlockSpec(memory_space=pltpu.HBM)
    lanes2 = 2 * LANES
    return pl.pallas_call(
        functools.partial(kernel, sizes),
        out_shape=jax.ShapeDtypeStruct(terminal.shape, f32),
        in_specs=[hbm] * 7,
        out_specs=pl.BlockSpec(memory_space=pl.ANY),
        scratch_shapes=[
            pltpu.VMEM((NCOMP, CX, CZ, lanes2), f32),
            pltpu.VMEM((2 * NCOMP, 2, NXB, ZIN, LANES), f32),
            pltpu.VMEM((2, 2, NXB, ZBUF, LANES), f32),
            pltpu.VMEM((2, 2, NXB, ZBUF, LANES), f32),
            pltpu.VMEM((2, 2, NXB, ZBUF, LANES), f32),
            pltpu.VMEM((2, NCOMP, NXO, CZ, lanes2), f32),
            pltpu.VMEM((NCOMP, 2, HALO, CZ, lanes2), f32),
            pltpu.VMEM((NCOMP, 2, HALO, CZ, lanes2), f32),
            pltpu.VMEM((2, HALO, CZ, lanes2), f32),
            pltpu.VMEM((XB * ZBUF, lanes2), jnp.bfloat16),
            pltpu.VMEM((XB * ZBUF, lanes2), jnp.bfloat16),
            pltpu.VMEM((1, lanes2), f32),
            pltpu.VMEM((1, lanes2), f32),
            pltpu.VMEM((lanes2, lanes2), jnp.bfloat16),
            pltpu.VMEM((lanes2, lanes2), jnp.bfloat16),
            pltpu.VMEM((8, lanes2), f32),
            pltpu.VMEM((2, 8, LANES), f32),
            pltpu.VMEM((8, LANES), f32),
            pltpu.VMEM((3, 8, LANES), f32),
            pltpu.VMEM((8, LANES), f32),
            pltpu.VMEM((nz - 1, 8, LANES), f32),
            dma((4 * NCOMP,)),
            dma((4,)),
            dma((NCOMP * NCH,)),
            dma((NCOMP * NCH,)),
            dma((NCOMP * 2,)),
            dma((NCOMP * 2,)),
            dma((NCOMP * NCH * 2,)),
            dma((NCOMP * NCH * 2,)),
            dma((3,)),
            dma((3,)),
            dma((nz - 1,)),
            dma((nz - 1,)),
            dma((NCOMP,)),
            dma((NCOMP,)),
            dma((2,)),
            dma((2,)),
            dma((3 * NCOMP,)),
        ],
        compiler_params=pltpu.CompilerParams(
            collective_id=0, has_side_effects=True, vmem_limit_bytes=50 * 1024 * 1024
        ),
    )(*(
        pltpu.with_memory_space_constraint(value, pltpu.HBM)
        for value in (
            terminal, jump, tangent,
            base_velocity.reshape(1, -1), base_shear.reshape(1, -1),
            jnp.asarray(high), jnp.asarray(low),
        )
    ))


def solution(mesh):
    sizes = tuple(mesh.shape[name] for name in ("seg", "gx", "gz"))
    split = P("seg", None, "gx", "gz", None)
    return jax.shard_map(
        functools.partial(shards, sizes),
        mesh=mesh,
        in_specs=(split, split, split, P(), P()),
        out_specs=split,
        check_vma=False,
    )
```

```python
import functools

import jax
import jax.numpy as jnp
import ml_dtypes
import numpy as np
from jax import lax
from jax.experimental import pallas as pl
from jax.experimental.pallas import tpu as pltpu
from jax.sharding import PartitionSpec as P

TIME_STEP = 0.15
DIFFUSE = 0.1
WALL_COEF = 0.0002
EPSILON = 1e-06
NEWTON_TURNS = 100
MESH = pl.DeviceIdType.MESH

NCOMP = 3
CX = 64
CZ = 16
LANES = 128
HALO = 8
XB = 16
NXO = CX + 2 * HALO
NXB = NXO + 4
ZIN = 40
ZBUF = 32
ZOUT = (32, 24, 24, 16)
CHUNK = 8
NCH = CX // CHUNK
AHEAD = 5
LAG = 2


def invert_newton(matrix):
    order = matrix.shape[0]
    identity = np.eye(order)
    scale_one = np.max(np.sum(np.abs(matrix), axis=0))
    scale_inf = np.max(np.sum(np.abs(matrix), axis=1))
    approx = matrix.T / (scale_one * scale_inf)
    for turn_index in range(NEWTON_TURNS):
        approx = approx @ (2.0 * identity - matrix @ approx)
    return approx


def wall_table(points):
    intervals = points - 1
    cheb_nodes = np.cos(np.pi * np.arange(points) / intervals)
    weights = np.ones(points)
    weights[0] = 2.0
    weights[-1] = 2.0
    weights = weights * (-1.0) ** np.arange(points)
    spread = cheb_nodes[:, None] - cheb_nodes[None, :]
    first_deriv = weights[:, None] / weights[None, :] / (spread + np.eye(points))
    first_deriv = first_deriv - np.eye(points) * first_deriv.sum(axis=1)[:, None]
    second = first_deriv @ first_deriv
    interior = np.eye(points - 2) - WALL_COEF * second[1:-1, 1:-1]
    helm_table = np.zeros((points, points))
    helm_table[1:-1, 1:-1] = invert_newton(interior)
    return helm_table.T.astype(np.float32)


def kernel(
    sizes,
    t_hbm, j_hbm, tan_hbm, vel_hbm, shear_hbm, hhi_hbm, hlo_hbm,
    out_hbm,
    tb, b0, w1, w2, w3, res, osend, orecv, oraw, ehi, elo, vel_ref, shear_ref, hhi_ref, hlo_ref, coef_ref, acc, ar_send, ar_recv_a, ar_mid, ar_recv_b,
    load_sem, const_sem, t_send, t_recv, zs_send, zs_recv, zt_send, zt_recv,
    ra_send, ra_recv, rb_send, rb_recv, o_send, o_recv, or_send, or_recv, out_sem,
):
    nseg, ngx, ngz = sizes
    seg, gx, gz = lax.axis_index("seg"), lax.axis_index("gx"), lax.axis_index("gz")
    nz = ngz // 2
    zc, core = gz // 2, lax.rem(gz, 2)
    before, after = lax.rem(seg + nseg - 1, nseg), lax.rem(seg + 1, nseg)
    zl, zr = lax.rem(gz + ngz - 1, ngz), lax.rem(gz + 1, ngz)
    ogx, ogz = 1 - gx, zc * 2 + (1 - core)
    left, right, partner = (seg, gx, zl), (seg, gx, zr), (seg, ogx, gz)
    group_a = [(seg, gx, ogz), (seg, ogx, gz), (seg, ogx, ogz)]
    group_b = [(seg, gx, lax.rem(zc + o, nz) * 2 + core) for o in range(1, nz)]
    outer = (seg, gx, lax.rem(gz + jnp.where(core == 0, ngz - 1, 1), ngz))

    def loads(start):
        for i, (src, dst) in enumerate((
            (vel_hbm, vel_ref), (shear_hbm, shear_ref), (hhi_hbm, hhi_ref), (hlo_hbm, hlo_ref),
        )):
            cp = pltpu.make_async_copy(src, dst, const_sem.at[i])
            if start:
                cp.start()
            else:
                cp.wait()
        for a, src in ((0, tan_hbm), (1, j_hbm)):
            for c in range(NCOMP):
                for h in range(2):
                    cp = pltpu.make_async_copy(
                        src.at[0, c, :, :, pl.ds(h * LANES, LANES)],
                        b0.at[a * NCOMP + c, h, pl.ds(2 + HALO, CX), pl.ds(HALO, CZ), :],
                        load_sem.at[(a * NCOMP + c) * 2 + h],
                    )
                    if start:
                        cp.start()
                    else:
                        cp.wait()

    barrier = pltpu.get_barrier_semaphore()
    peers = [(before, gx, gz), (after, gx, gz), outer] + group_a + group_b
    for d in peers:
        pl.semaphore_signal(barrier, inc=1, device_id=d, device_id_type=MESH)
    loads(True)
    pl.semaphore_wait(barrier, len(peers))

    def t_copy(c, i):
        rows = pl.ds(i * CHUNK, CHUNK)
        return pltpu.make_async_remote_copy(
            src_ref=t_hbm.at[0, c, rows],
            dst_ref=tb.at[c, rows],
            send_sem=t_send.at[c * NCH + i],
            recv_sem=t_recv.at[c * NCH + i],
            device_id=(before, gx, gz),
            device_id_type=MESH,
        )

    for i in range(AHEAD):
        t_copy(i // NCH, i % NCH).start()

    def zero_pads(s, _):
        for h in range(2):
            for lo, hi in ((0, 2 + HALO), (2 + HALO + CX, NXB)):
                b0[s, h, lo:hi, :, :] = jnp.zeros((hi - lo, ZIN, LANES), jnp.float32)
            b0[s, h, 2 + HALO:2 + HALO + CX, 2 * HALO + CZ:, :] = jnp.zeros(
                (CX, ZIN - 2 * HALO - CZ, LANES), jnp.float32)
        return 0

    lax.fori_loop(0, 2 * NCOMP, zero_pads, 0)
    for w in (w1, w2, w3):
        for s in range(2):
            for h in range(2):
                for lo in (0, NXB - 2):
                    w[s, h, lo:lo + 2, :, :] = jnp.zeros((2, ZBUF, LANES), jnp.float32)
                w[s, h, 2:NXB - 2, 24:, :] = jnp.zeros((NXB - 4, 8, LANES), jnp.float32)
    acc[...] = jnp.zeros_like(acc)
    def strip(slot, x0, nx, side, send_sem, recv_sem):
        rows = pl.ds(2 + HALO + x0, nx)
        src = pl.ds(HALO, HALO) if side == 0 else pl.ds(HALO + CZ - HALO, HALO)
        dst = pl.ds(HALO + CZ, HALO) if side == 0 else pl.ds(0, HALO)
        return pltpu.make_async_remote_copy(
            src_ref=b0.at[slot, :, rows, src, :],
            dst_ref=b0.at[slot, :, rows, dst, :],
            send_sem=send_sem,
            recv_sem=recv_sem,
            device_id=left if side == 0 else right,
            device_id_type=MESH,
        )

    def tan_strip(c, side):
        k = c * 2 + side
        return strip(c, 0, CX, side, zs_send.at[k], zs_recv.at[k])

    def start_strip(c, i, side):
        k = (c * NCH + i) * 2 + side
        return strip(NCOMP + c, i * CHUNK, CHUNK, side, zt_send.at[k], zt_recv.at[k])

    loads(False)
    near, far = DIFFUSE * 16.0 / 12.0, DIFFUSE / 12.0
    push = TIME_STEP * vel_ref[...]
    coef_ref[0:1, :] = push * (8.0 / 12.0) + near
    coef_ref[1:2, :] = push * (-8.0 / 12.0) + near
    coef_ref[2:3, :] = push * (-1.0 / 12.0) - far
    coef_ref[3:4, :] = push * (1.0 / 12.0) - far
    coef_ref[4:5, :] = -TIME_STEP * shear_ref[...]
    for side in range(2):
        tan_strip(0, side).start()

    def dot_rows(first, second):
        prod = first * second
        return jnp.sum(prod.reshape(-1, 8, LANES), axis=0)

    def square(i, _):
        c, x = i // NCH, lax.rem(i, NCH) * CHUNK
        for h in range(2):
            tau = b0[c, h, pl.ds(2 + HALO + x, CHUNK), HALO:HALO + CZ, :]
            acc[1] += dot_rows(tau, tau)
        return 0

    lax.fori_loop(0, NCOMP * NCH, square, 0)

    def piece(j):
        c, i = j // NCH, lax.rem(j, NCH)
        t_copy(c, i).wait_recv()
        rows = pl.ds(2 + HALO + i * CHUNK, CHUNK)
        for h in range(2):
            started = b0[NCOMP + c, h, rows, HALO:HALO + CZ, :] + tb[
                c, pl.ds(i * CHUNK, CHUNK), :, h * LANES:(h + 1) * LANES]
            b0[NCOMP + c, h, rows, HALO:HALO + CZ, :] = started
            acc[0] += dot_rows(started, b0[c, h, rows, HALO:HALO + CZ, :])
        start_strip(c, i, 0).start()
        start_strip(c, i, 1).start()

    def reduce_a(o):
        return pltpu.make_async_remote_copy(
            src_ref=ar_send, dst_ref=ar_recv_a.at[o], send_sem=ra_send.at[o], recv_sem=ra_recv.at[o],
            device_id=group_a[o], device_id_type=MESH)

    def reduce_b(o):
        return pltpu.make_async_remote_copy(
            src_ref=ar_mid, dst_ref=ar_recv_b.at[o], send_sem=rb_send.at[o], recv_sem=rb_recv.at[o],
            device_id=group_b[o], device_id_type=MESH)

    def outflow(c):
        sides = pl.ds(1, 1) if c == 0 else pl.ds(0, 2)
        return pltpu.make_async_remote_copy(
            src_ref=osend.at[c, sides], dst_ref=orecv.at[c, sides],
            send_sem=o_send.at[c], recv_sem=o_recv.at[c],
            device_id=partner, device_id_type=MESH)

    def raw_outflow(a):
        return pltpu.make_async_remote_copy(
            src_ref=res.at[a, 0, pl.ds(HALO + CX, HALO)], dst_ref=oraw.at[a],
            send_sem=or_send.at[a], recv_sem=or_recv.at[a],
            device_id=partner, device_id_type=MESH)

    def reduce_all():
        row = lax.broadcasted_iota(jnp.int32, (8, LANES), 0)
        top = jnp.sum(acc[0], axis=0, keepdims=True)
        low = jnp.sum(acc[1], axis=0, keepdims=True)
        ar_send[...] = jnp.where(row == 0, top, jnp.where(row == 1, low, 0.0))
        for o in range(3):
            reduce_a(o).start()
        for o in range(3):
            reduce_a(o).wait_recv()
        ar_mid[...] = ar_send[...] + ar_recv_a[0] + (ar_recv_a[1] + ar_recv_a[2])
        for o in range(nz - 1):
            reduce_b(o).start()
        for o in range(nz - 1):
            reduce_b(o).wait_recv()
        total = ar_mid[...]
        for o in range(nz - 1):
            total += ar_recv_b[o]
        sums = jnp.sum(total, axis=1, keepdims=True)
        acc[0] = jnp.broadcast_to(sums[0:1] / (sums[1:2] + EPSILON), (8, LANES))

    def send_outflow(c):
        along = acc[0, 0:1, 0:1]

        for side, at in ((0, HALO + CX), (1, 0)):
            if c > 0 or side > 0:
                osend[c, side] = res[1, c, at:at + HALO] - along * res[0, c, at:at + HALO]
        outflow(c).start()

    bufs = (b0, w1, w2, w3)

    def advance(k, n, a, c, first, count, sheared):
        half_set = jnp.minimum(c, 1)
        z = ZOUT[k]
        m = count * z
        src = bufs[k]
        slot = n if k == 0 else half_set
        slot0 = a * NCOMP if k == 0 else 0
        for h in range(2):
            cols = slice(h * LANES, (h + 1) * LANES)
            cs = [coef_ref[r:r + 1, cols] for r in range(5)]
            rows = {}

            def row(i):
                if i not in rows:
                    rows[i] = src[slot, h, first + i, 2:2 + z, :]
                return rows[i]

            for p in range(count // 2):
                both = []
                for i in (2 * p, 2 * p + 1):

                    def at(dz):
                        return src[slot, h, first + i + 2, 2 + dz:2 + dz + z, :]

                    e = 0.5 * row(i + 2)
                    e += (DIFFUSE * 16.0 / 12.0) * (at(1) + at(-1))
                    e += (-DIFFUSE / 12.0) * (at(2) + at(-2))
                    e += cs[0] * row(i + 3) + cs[1] * row(i + 1)
                    e += cs[2] * row(i + 4) + cs[3] * row(i)
                    if sheared:
                        e += cs[4] * src[slot0, h, first + i + 2, 2:2 + z, :]
                    both.append(e)
                e = jnp.concatenate(both, axis=0)
                hi = e.astype(jnp.bfloat16)
                ehi[2 * p * z:2 * (p + 1) * z, cols] = hi
                elo[2 * p * z:2 * (p + 1) * z, cols] = (e - hi.astype(jnp.float32)).astype(jnp.bfloat16)
        high = ehi[:m]
        out = jnp.dot(
            jnp.concatenate([high, elo[:m], high], axis=1),
            jnp.concatenate([hhi_ref[...], hhi_ref[...], hlo_ref[...]], axis=0),
            preferred_element_type=jnp.float32,
        )
        if k < 3:
            for h in range(2):
                bufs[k + 1][half_set, h, pl.ds(2 + first, count), 0:z, :] = out[
                    :, h * LANES:(h + 1) * LANES].reshape(count, z, LANES)
        else:
            res[a, c, pl.ds(first, count)] = out.reshape(count, z, 2 * LANES)

    def steps(n, a, c, sheared):
        for k in range(4):
            def block(b, _):
                advance(k, n, a, c, b * XB, XB, sheared)
                return 0

            lax.fori_loop(0, NXO // XB, block, 0)
            sent = n * 4 + k

            @pl.when(sent < NCOMP * NCH - AHEAD)
            def _():
                later = sent + AHEAD
                t_copy(later // NCH, lax.rem(later, NCH)).start()

            early = (sent >= 16) & (sent < 16 + LAG)

            @pl.when((sent >= LAG) & jnp.logical_not(early) & (n < 2 * NCOMP - 1))
            def _():
                piece(sent - LAG)

    def item(n, _):
        a, c = n // NCOMP, lax.rem(n, NCOMP)

        @pl.when(a == 0)
        def _():
            for side in range(2):
                tan_strip(c, side).wait_recv()

        @pl.when(n < NCOMP - 1)
        def _():
            for side in range(2):
                tan_strip(n + 1, side).start()

        @pl.when(n == 2 * NCOMP - 2)
        def _():
            for j in range(NCH * 2 - LAG, NCH * 2):
                piece(jnp.int32(j))

        @pl.when(n == 2 * NCOMP - 1)
        def _():
            def last(j, _):
                piece(j)
                return 0

            lax.fori_loop(20 - LAG, NCOMP * NCH, last, 0)
            for d in range(2):
                raw_outflow(d).start()
            reduce_all()
            for d in range(NCOMP - 1):
                send_outflow(d)

        @pl.when(a == 1)
        def _():
            def strips(i, _):
                start_strip(c, i, 0).wait_recv()
                start_strip(c, i, 1).wait_recv()
                return 0

            lax.fori_loop(0, NCH, strips, 0)

        @pl.when(n == 2 * NCOMP - 1)
        def _():
            for k in range(4):
                def edge(e, _):
                    advance(k, n, a, c, HALO - 2 * (k + 1) + e * (CX + 4 * (k + 1) - HALO), HALO, False)
                    return 0

                lax.fori_loop(0, 2, edge, 0)
            send_outflow(NCOMP - 1)

        @pl.when(c == 1)
        def _():
            steps(n, a, c, True)

        @pl.when(c != 1)
        def _():
            steps(n, a, c, False)
        return 0

    lax.fori_loop(0, 2 * NCOMP, item, 0)
    along = acc[0, 0:1, 0:1]

    def write(c, lo, n, k):
        return pltpu.make_async_copy(
            tb.at[c, pl.ds(lo, n)], out_hbm.at[0, c, pl.ds(lo, n)], out_sem.at[c * 3 + k])

    inner = CX - 2 * HALO
    for c in range(NCOMP):
        def mix(i, _):
            rows = pl.ds(2 * HALO + i * HALO, HALO)
            tb[c, pl.ds(HALO + i * HALO, HALO)] = res[1, c, rows] - along * res[0, c, rows]
            return 0

        lax.fori_loop(0, inner // HALO, mix, 0)
        write(c, HALO, inner, 0).start()
    for d in range(2):
        raw_outflow(d).wait_recv()
    for c in range(NCOMP):
        outflow(c).wait_recv()
        for side, at in ((0, 0), (1, CX - HALO)):
            own = res[1, c, HALO + at:2 * HALO + at] - along * res[0, c, HALO + at:2 * HALO + at]
            if c == 0 and side == 0:
                other = oraw[1] - along * oraw[0]
            else:
                other = orecv[c, side]
            tb[c, at:at + HALO] = own + other
        write(c, 0, HALO, 1).start()
        write(c, CX - HALO, HALO, 2).start()

    for c in range(NCOMP):
        write(c, HALO, inner, 0).wait()
        write(c, 0, HALO, 1).wait()
        write(c, CX - HALO, HALO, 2).wait()
        outflow(c).wait_send()
        for side in range(2):
            tan_strip(c, side).wait_send()

        @pl.loop(0, NCH)
        def _(i):
            t_copy(c, i).wait_send()
            start_strip(c, i, 0).wait_send()
            start_strip(c, i, 1).wait_send()
    for d in range(2):
        raw_outflow(d).wait_send()
    for o in range(3):
        reduce_a(o).wait_send()
    for o in range(nz - 1):
        reduce_b(o).wait_send()


def shards(sizes, terminal, jump, tangent, base_velocity, base_shear):
    table = wall_table(base_velocity.shape[0])
    high = table.astype(ml_dtypes.bfloat16)
    low = (table - high.astype(np.float32)).astype(ml_dtypes.bfloat16)
    nz = sizes[2] // 2
    f32 = jnp.float32
    dma = pltpu.SemaphoreType.DMA
    hbm = pl.BlockSpec(memory_space=pltpu.HBM)
    lanes2 = 2 * LANES
    return pl.pallas_call(
        functools.partial(kernel, sizes),
        out_shape=jax.ShapeDtypeStruct(terminal.shape, f32),
        in_specs=[hbm] * 7,
        out_specs=pl.BlockSpec(memory_space=pl.ANY),
        scratch_shapes=[
            pltpu.VMEM((NCOMP, CX, CZ, lanes2), f32),
            pltpu.VMEM((2 * NCOMP, 2, NXB, ZIN, LANES), f32),
            pltpu.VMEM((2, 2, NXB, ZBUF, LANES), f32),
            pltpu.VMEM((2, 2, NXB, ZBUF, LANES), f32),
            pltpu.VMEM((2, 2, NXB, ZBUF, LANES), f32),
            pltpu.VMEM((2, NCOMP, NXO, CZ, lanes2), f32),
            pltpu.VMEM((NCOMP, 2, HALO, CZ, lanes2), f32),
            pltpu.VMEM((NCOMP, 2, HALO, CZ, lanes2), f32),
            pltpu.VMEM((2, HALO, CZ, lanes2), f32),
            pltpu.VMEM((XB * ZBUF, lanes2), jnp.bfloat16),
            pltpu.VMEM((XB * ZBUF, lanes2), jnp.bfloat16),
            pltpu.VMEM((1, lanes2), f32),
            pltpu.VMEM((1, lanes2), f32),
            pltpu.VMEM((lanes2, lanes2), jnp.bfloat16),
            pltpu.VMEM((lanes2, lanes2), jnp.bfloat16),
            pltpu.VMEM((8, lanes2), f32),
            pltpu.VMEM((2, 8, LANES), f32),
            pltpu.VMEM((8, LANES), f32),
            pltpu.VMEM((3, 8, LANES), f32),
            pltpu.VMEM((8, LANES), f32),
            pltpu.VMEM((nz - 1, 8, LANES), f32),
            dma((4 * NCOMP,)),
            dma((4,)),
            dma((NCOMP * NCH,)),
            dma((NCOMP * NCH,)),
            dma((NCOMP * 2,)),
            dma((NCOMP * 2,)),
            dma((NCOMP * NCH * 2,)),
            dma((NCOMP * NCH * 2,)),
            dma((3,)),
            dma((3,)),
            dma((nz - 1,)),
            dma((nz - 1,)),
            dma((NCOMP,)),
            dma((NCOMP,)),
            dma((2,)),
            dma((2,)),
            dma((3 * NCOMP,)),
        ],
        compiler_params=pltpu.CompilerParams(
            collective_id=0, has_side_effects=True, vmem_limit_bytes=50 * 1024 * 1024
        ),
    )(*(
        pltpu.with_memory_space_constraint(value, pltpu.HBM)
        for value in (
            terminal, jump, tangent,
            base_velocity.reshape(1, -1), base_shear.reshape(1, -1),
            jnp.asarray(high), jnp.asarray(low),
        )
    ))


def solution(mesh):
    sizes = tuple(mesh.shape[name] for name in ("seg", "gx", "gz"))
    split = P("seg", None, "gx", "gz", None)
    return jax.shard_map(
        functools.partial(shards, sizes),
        mesh=mesh,
        in_specs=(split, split, split, P(), P()),
        out_specs=split,
        check_vma=False,
    )
```

```python
import functools

import jax
import jax.numpy as jnp
import ml_dtypes
import numpy as np
from jax import lax
from jax.experimental import pallas as pl
from jax.experimental.pallas import tpu as pltpu
from jax.sharding import PartitionSpec as P

TIME_STEP = 0.15
DIFFUSE = 0.1
WALL_COEF = 0.0002
EPSILON = 1e-06
NEWTON_TURNS = 100
MESH = pl.DeviceIdType.MESH

NCOMP = 3
CX = 64
CZ = 16
LANES = 128
HALO = 8
XB = 16
NXO = CX + 2 * HALO
NXB = NXO + 4
ZIN = 40
ZBUF = 32
ZOUT = (32, 24, 24, 16)
CHUNK = 8
NCH = CX // CHUNK
AHEAD = 7
LAG = 3


def invert_newton(matrix):
    order = matrix.shape[0]
    identity = np.eye(order)
    scale_one = np.max(np.sum(np.abs(matrix), axis=0))
    scale_inf = np.max(np.sum(np.abs(matrix), axis=1))
    approx = matrix.T / (scale_one * scale_inf)
    for turn_index in range(NEWTON_TURNS):
        approx = approx @ (2.0 * identity - matrix @ approx)
    return approx


def wall_table(points):
    intervals = points - 1
    cheb_nodes = np.cos(np.pi * np.arange(points) / intervals)
    weights = np.ones(points)
    weights[0] = 2.0
    weights[-1] = 2.0
    weights = weights * (-1.0) ** np.arange(points)
    spread = cheb_nodes[:, None] - cheb_nodes[None, :]
    first_deriv = weights[:, None] / weights[None, :] / (spread + np.eye(points))
    first_deriv = first_deriv - np.eye(points) * first_deriv.sum(axis=1)[:, None]
    second = first_deriv @ first_deriv
    interior = np.eye(points - 2) - WALL_COEF * second[1:-1, 1:-1]
    helm_table = np.zeros((points, points))
    helm_table[1:-1, 1:-1] = invert_newton(interior)
    return helm_table.T.astype(np.float32)


def kernel(
    sizes,
    t_hbm, j_hbm, tan_hbm, vel_hbm, shear_hbm, hhi_hbm, hlo_hbm,
    out_hbm,
    tb, b0, w1, w2, w3, res, osend, orecv, oraw, ehi, elo, vel_ref, shear_ref, hhi_ref, hlo_ref, coef_ref, acc, ar_send, ar_recv_a, ar_mid, ar_recv_b,
    load_sem, const_sem, t_send, t_recv, zs_send, zs_recv, zt_send, zt_recv,
    ra_send, ra_recv, rb_send, rb_recv, o_send, o_recv, or_send, or_recv, out_sem,
):
    nseg, ngx, ngz = sizes
    seg, gx, gz = lax.axis_index("seg"), lax.axis_index("gx"), lax.axis_index("gz")
    nz = ngz // 2
    zc, core = gz // 2, lax.rem(gz, 2)
    before, after = lax.rem(seg + nseg - 1, nseg), lax.rem(seg + 1, nseg)
    zl, zr = lax.rem(gz + ngz - 1, ngz), lax.rem(gz + 1, ngz)
    ogx, ogz = 1 - gx, zc * 2 + (1 - core)
    left, right, partner = (seg, gx, zl), (seg, gx, zr), (seg, ogx, gz)
    group_a = [(seg, gx, ogz), (seg, ogx, gz), (seg, ogx, ogz)]
    group_b = [(seg, gx, lax.rem(zc + o, nz) * 2 + core) for o in range(1, nz)]
    outer = (seg, gx, lax.rem(gz + jnp.where(core == 0, ngz - 1, 1), ngz))

    def loads(start):
        for i, (src, dst) in enumerate((
            (vel_hbm, vel_ref), (shear_hbm, shear_ref), (hhi_hbm, hhi_ref), (hlo_hbm, hlo_ref),
        )):
            cp = pltpu.make_async_copy(src, dst, const_sem.at[i])
            if start:
                cp.start()
            else:
                cp.wait()
        for a, src in ((0, tan_hbm), (1, j_hbm)):
            for c in range(NCOMP):
                for h in range(2):
                    cp = pltpu.make_async_copy(
                        src.at[0, c, :, :, pl.ds(h * LANES, LANES)],
                        b0.at[a * NCOMP + c, h, pl.ds(2 + HALO, CX), pl.ds(HALO, CZ), :],
                        load_sem.at[(a * NCOMP + c) * 2 + h],
                    )
                    if start:
                        cp.start()
                    else:
                        cp.wait()

    barrier = pltpu.get_barrier_semaphore()
    peers = [(before, gx, gz), (after, gx, gz), outer] + group_a + group_b
    for d in peers:
        pl.semaphore_signal(barrier, inc=1, device_id=d, device_id_type=MESH)
    loads(True)
    pl.semaphore_wait(barrier, len(peers))

    def t_copy(c, i):
        rows = pl.ds(i * CHUNK, CHUNK)
        return pltpu.make_async_remote_copy(
            src_ref=t_hbm.at[0, c, rows],
            dst_ref=tb.at[c, rows],
            send_sem=t_send.at[c * NCH + i],
            recv_sem=t_recv.at[c * NCH + i],
            device_id=(before, gx, gz),
            device_id_type=MESH,
        )

    for i in range(AHEAD):
        t_copy(i // NCH, i % NCH).start()

    def zero_pads(s, _):
        for h in range(2):
            for lo, hi in ((0, 2 + HALO), (2 + HALO + CX, NXB)):
                b0[s, h, lo:hi, :, :] = jnp.zeros((hi - lo, ZIN, LANES), jnp.float32)
            b0[s, h, 2 + HALO:2 + HALO + CX, 2 * HALO + CZ:, :] = jnp.zeros(
                (CX, ZIN - 2 * HALO - CZ, LANES), jnp.float32)
        return 0

    lax.fori_loop(0, 2 * NCOMP, zero_pads, 0)
    for w in (w1, w2, w3):
        for s in range(2):
            for h in range(2):
                for lo in (0, NXB - 2):
                    w[s, h, lo:lo + 2, :, :] = jnp.zeros((2, ZBUF, LANES), jnp.float32)
                w[s, h, 2:NXB - 2, 24:, :] = jnp.zeros((NXB - 4, 8, LANES), jnp.float32)
    acc[...] = jnp.zeros_like(acc)
    def strip(slot, x0, nx, side, send_sem, recv_sem):
        rows = pl.ds(2 + HALO + x0, nx)
        src = pl.ds(HALO, HALO) if side == 0 else pl.ds(HALO + CZ - HALO, HALO)
        dst = pl.ds(HALO + CZ, HALO) if side == 0 else pl.ds(0, HALO)
        return pltpu.make_async_remote_copy(
            src_ref=b0.at[slot, :, rows, src, :],
            dst_ref=b0.at[slot, :, rows, dst, :],
            send_sem=send_sem,
            recv_sem=recv_sem,
            device_id=left if side == 0 else right,
            device_id_type=MESH,
        )

    def tan_strip(c, side):
        k = c * 2 + side
        return strip(c, 0, CX, side, zs_send.at[k], zs_recv.at[k])

    def start_strip(c, i, side):
        k = (c * NCH + i) * 2 + side
        return strip(NCOMP + c, i * CHUNK, CHUNK, side, zt_send.at[k], zt_recv.at[k])

    loads(False)
    near, far = DIFFUSE * 16.0 / 12.0, DIFFUSE / 12.0
    push = TIME_STEP * vel_ref[...]
    coef_ref[0:1, :] = push * (8.0 / 12.0) + near
    coef_ref[1:2, :] = push * (-8.0 / 12.0) + near
    coef_ref[2:3, :] = push * (-1.0 / 12.0) - far
    coef_ref[3:4, :] = push * (1.0 / 12.0) - far
    coef_ref[4:5, :] = -TIME_STEP * shear_ref[...]
    for side in range(2):
        tan_strip(0, side).start()

    def dot_rows(first, second):
        prod = first * second
        return jnp.sum(prod.reshape(-1, 8, LANES), axis=0)

    def square(i, _):
        c, x = i // NCH, lax.rem(i, NCH) * CHUNK
        for h in range(2):
            tau = b0[c, h, pl.ds(2 + HALO + x, CHUNK), HALO:HALO + CZ, :]
            acc[1] += dot_rows(tau, tau)
        return 0

    lax.fori_loop(0, NCOMP * NCH, square, 0)

    def piece(j):
        c, i = j // NCH, lax.rem(j, NCH)
        t_copy(c, i).wait_recv()
        rows = pl.ds(2 + HALO + i * CHUNK, CHUNK)
        for h in range(2):
            started = b0[NCOMP + c, h, rows, HALO:HALO + CZ, :] + tb[
                c, pl.ds(i * CHUNK, CHUNK), :, h * LANES:(h + 1) * LANES]
            b0[NCOMP + c, h, rows, HALO:HALO + CZ, :] = started
            acc[0] += dot_rows(started, b0[c, h, rows, HALO:HALO + CZ, :])
        start_strip(c, i, 0).start()
        start_strip(c, i, 1).start()

    def reduce_a(o):
        return pltpu.make_async_remote_copy(
            src_ref=ar_send, dst_ref=ar_recv_a.at[o], send_sem=ra_send.at[o], recv_sem=ra_recv.at[o],
            device_id=group_a[o], device_id_type=MESH)

    def reduce_b(o):
        return pltpu.make_async_remote_copy(
            src_ref=ar_mid, dst_ref=ar_recv_b.at[o], send_sem=rb_send.at[o], recv_sem=rb_recv.at[o],
            device_id=group_b[o], device_id_type=MESH)

    def outflow(c):
        sides = pl.ds(1, 1) if c == 0 else pl.ds(0, 2)
        return pltpu.make_async_remote_copy(
            src_ref=osend.at[c, sides], dst_ref=orecv.at[c, sides],
            send_sem=o_send.at[c], recv_sem=o_recv.at[c],
            device_id=partner, device_id_type=MESH)

    def raw_outflow(a):
        return pltpu.make_async_remote_copy(
            src_ref=res.at[a, 0, pl.ds(HALO + CX, HALO)], dst_ref=oraw.at[a],
            send_sem=or_send.at[a], recv_sem=or_recv.at[a],
            device_id=partner, device_id_type=MESH)

    def reduce_all():
        row = lax.broadcasted_iota(jnp.int32, (8, LANES), 0)
        top = jnp.sum(acc[0], axis=0, keepdims=True)
        low = jnp.sum(acc[1], axis=0, keepdims=True)
        ar_send[...] = jnp.where(row == 0, top, jnp.where(row == 1, low, 0.0))
        for o in range(3):
            reduce_a(o).start()
        for d in range(2):
            raw_outflow(d).start()
        for o in range(3):
            reduce_a(o).wait_recv()
        ar_mid[...] = ar_send[...] + ar_recv_a[0] + (ar_recv_a[1] + ar_recv_a[2])
        for o in range(nz - 1):
            reduce_b(o).start()
        for o in range(nz - 1):
            reduce_b(o).wait_recv()
        total = ar_mid[...]
        for o in range(nz - 1):
            total += ar_recv_b[o]
        sums = jnp.sum(total, axis=1, keepdims=True)
        acc[0] = jnp.broadcast_to(sums[0:1] / (sums[1:2] + EPSILON), (8, LANES))

    def send_outflow(c):
        along = acc[0, 0:1, 0:1]

        for side, at in ((0, HALO + CX), (1, 0)):
            if c > 0 or side > 0:
                osend[c, side] = res[1, c, at:at + HALO] - along * res[0, c, at:at + HALO]
        outflow(c).start()

    bufs = (b0, w1, w2, w3)

    def advance(k, n, a, c, first, count, sheared):
        half_set = jnp.minimum(c, 1)
        z = ZOUT[k]
        m = count * z
        src = bufs[k]
        slot = n if k == 0 else half_set
        slot0 = a * NCOMP if k == 0 else 0
        for h in range(2):
            cols = slice(h * LANES, (h + 1) * LANES)
            cs = [coef_ref[r:r + 1, cols] for r in range(5)]
            rows = {}

            def row(i):
                if i not in rows:
                    rows[i] = src[slot, h, first + i, 2:2 + z, :]
                return rows[i]

            for p in range(count // 2):
                both = []
                for i in (2 * p, 2 * p + 1):

                    def at(dz):
                        return src[slot, h, first + i + 2, 2 + dz:2 + dz + z, :]

                    e = 0.5 * row(i + 2)
                    e += (DIFFUSE * 16.0 / 12.0) * (at(1) + at(-1))
                    e += (-DIFFUSE / 12.0) * (at(2) + at(-2))
                    e += cs[0] * row(i + 3) + cs[1] * row(i + 1)
                    e += cs[2] * row(i + 4) + cs[3] * row(i)
                    if sheared:
                        e += cs[4] * src[slot0, h, first + i + 2, 2:2 + z, :]
                    both.append(e)
                e = jnp.concatenate(both, axis=0)
                hi = e.astype(jnp.bfloat16)
                ehi[2 * p * z:2 * (p + 1) * z, cols] = hi
                elo[2 * p * z:2 * (p + 1) * z, cols] = (e - hi.astype(jnp.float32)).astype(jnp.bfloat16)
        high = ehi[:m]
        out = jnp.dot(
            jnp.concatenate([high, elo[:m], high], axis=1),
            jnp.concatenate([hhi_ref[...], hhi_ref[...], hlo_ref[...]], axis=0),
            preferred_element_type=jnp.float32,
        )
        if k < 3:
            for h in range(2):
                bufs[k + 1][half_set, h, pl.ds(2 + first, count), 0:z, :] = out[
                    :, h * LANES:(h + 1) * LANES].reshape(count, z, LANES)
        else:
            res[a, c, pl.ds(first, count)] = out.reshape(count, z, 2 * LANES)

    def steps(n, a, c, sheared):
        for k in range(4):
            def block(b, _):
                advance(k, n, a, c, b * XB, XB, sheared)
                return 0

            lax.fori_loop(0, NXO // XB, block, 0)
            sent = n * 4 + k

            @pl.when(sent < NCOMP * NCH - AHEAD)
            def _():
                later = sent + AHEAD
                t_copy(later // NCH, lax.rem(later, NCH)).start()

            early = (sent >= 16) & (sent < 16 + LAG)

            @pl.when((sent >= LAG) & jnp.logical_not(early) & (n < 2 * NCOMP - 1))
            def _():
                piece(sent - LAG)

    def item(n, _):
        a, c = n // NCOMP, lax.rem(n, NCOMP)

        @pl.when(a == 0)
        def _():
            for side in range(2):
                tan_strip(c, side).wait_recv()

        @pl.when(n < NCOMP - 1)
        def _():
            for side in range(2):
                tan_strip(n + 1, side).start()

        @pl.when(n == 2 * NCOMP - 2)
        def _():
            for j in range(NCH * 2 - LAG, NCH * 2):
                piece(jnp.int32(j))

        @pl.when(n == 2 * NCOMP - 1)
        def _():
            def last(j, _):
                piece(j)
                return 0

            lax.fori_loop(20 - LAG, NCOMP * NCH, last, 0)
            reduce_all()
            for d in range(NCOMP - 1):
                send_outflow(d)

        @pl.when(a == 1)
        def _():
            def strips(i, _):
                start_strip(c, i, 0).wait_recv()
                start_strip(c, i, 1).wait_recv()
                return 0

            lax.fori_loop(0, NCH, strips, 0)

        @pl.when(n == 2 * NCOMP - 1)
        def _():
            for k in range(4):
                def edge(e, _):
                    advance(k, n, a, c, HALO - 2 * (k + 1) + e * (CX + 4 * (k + 1) - HALO), HALO, False)
                    return 0

                lax.fori_loop(0, 2, edge, 0)
            send_outflow(NCOMP - 1)

        @pl.when(c == 1)
        def _():
            steps(n, a, c, True)

        @pl.when(c != 1)
        def _():
            steps(n, a, c, False)
        return 0

    lax.fori_loop(0, 2 * NCOMP, item, 0)
    along = acc[0, 0:1, 0:1]

    def write(c, lo, n, k):
        return pltpu.make_async_copy(
            tb.at[c, pl.ds(lo, n)], out_hbm.at[0, c, pl.ds(lo, n)], out_sem.at[c * 3 + k])

    inner = CX - 2 * HALO
    for c in range(NCOMP):
        def mix(i, _):
            rows = pl.ds(2 * HALO + i * HALO, HALO)
            tb[c, pl.ds(HALO + i * HALO, HALO)] = res[1, c, rows] - along * res[0, c, rows]
            return 0

        lax.fori_loop(0, inner // HALO, mix, 0)
        write(c, HALO, inner, 0).start()
    for d in range(2):
        raw_outflow(d).wait_recv()
    for c in range(NCOMP):
        outflow(c).wait_recv()
        for side, at in ((0, 0), (1, CX - HALO)):
            own = res[1, c, HALO + at:2 * HALO + at] - along * res[0, c, HALO + at:2 * HALO + at]
            if c == 0 and side == 0:
                other = oraw[1] - along * oraw[0]
            else:
                other = orecv[c, side]
            tb[c, at:at + HALO] = own + other
        write(c, 0, HALO, 1).start()
        write(c, CX - HALO, HALO, 2).start()

    for c in range(NCOMP):
        write(c, HALO, inner, 0).wait()
        write(c, 0, HALO, 1).wait()
        write(c, CX - HALO, HALO, 2).wait()
        outflow(c).wait_send()
        for side in range(2):
            tan_strip(c, side).wait_send()

        @pl.loop(0, NCH)
        def _(i):
            t_copy(c, i).wait_send()
            start_strip(c, i, 0).wait_send()
            start_strip(c, i, 1).wait_send()
    for d in range(2):
        raw_outflow(d).wait_send()
    for o in range(3):
        reduce_a(o).wait_send()
    for o in range(nz - 1):
        reduce_b(o).wait_send()


def shards(sizes, terminal, jump, tangent, base_velocity, base_shear):
    table = wall_table(base_velocity.shape[0])
    high = table.astype(ml_dtypes.bfloat16)
    low = (table - high.astype(np.float32)).astype(ml_dtypes.bfloat16)
    nz = sizes[2] // 2
    f32 = jnp.float32
    dma = pltpu.SemaphoreType.DMA
    hbm = pl.BlockSpec(memory_space=pltpu.HBM)
    lanes2 = 2 * LANES
    return pl.pallas_call(
        functools.partial(kernel, sizes),
        out_shape=jax.ShapeDtypeStruct(terminal.shape, f32),
        in_specs=[hbm] * 7,
        out_specs=pl.BlockSpec(memory_space=pl.ANY),
        scratch_shapes=[
            pltpu.VMEM((NCOMP, CX, CZ, lanes2), f32),
            pltpu.VMEM((2 * NCOMP, 2, NXB, ZIN, LANES), f32),
            pltpu.VMEM((2, 2, NXB, ZBUF, LANES), f32),
            pltpu.VMEM((2, 2, NXB, ZBUF, LANES), f32),
            pltpu.VMEM((2, 2, NXB, ZBUF, LANES), f32),
            pltpu.VMEM((2, NCOMP, NXO, CZ, lanes2), f32),
            pltpu.VMEM((NCOMP, 2, HALO, CZ, lanes2), f32),
            pltpu.VMEM((NCOMP, 2, HALO, CZ, lanes2), f32),
            pltpu.VMEM((2, HALO, CZ, lanes2), f32),
            pltpu.VMEM((XB * ZBUF, lanes2), jnp.bfloat16),
            pltpu.VMEM((XB * ZBUF, lanes2), jnp.bfloat16),
            pltpu.VMEM((1, lanes2), f32),
            pltpu.VMEM((1, lanes2), f32),
            pltpu.VMEM((lanes2, lanes2), jnp.bfloat16),
            pltpu.VMEM((lanes2, lanes2), jnp.bfloat16),
            pltpu.VMEM((8, lanes2), f32),
            pltpu.VMEM((2, 8, LANES), f32),
            pltpu.VMEM((8, LANES), f32),
            pltpu.VMEM((3, 8, LANES), f32),
            pltpu.VMEM((8, LANES), f32),
            pltpu.VMEM((nz - 1, 8, LANES), f32),
            dma((4 * NCOMP,)),
            dma((4,)),
            dma((NCOMP * NCH,)),
            dma((NCOMP * NCH,)),
            dma((NCOMP * 2,)),
            dma((NCOMP * 2,)),
            dma((NCOMP * NCH * 2,)),
            dma((NCOMP * NCH * 2,)),
            dma((3,)),
            dma((3,)),
            dma((nz - 1,)),
            dma((nz - 1,)),
            dma((NCOMP,)),
            dma((NCOMP,)),
            dma((2,)),
            dma((2,)),
            dma((3 * NCOMP,)),
        ],
        compiler_params=pltpu.CompilerParams(
            collective_id=0, has_side_effects=True, vmem_limit_bytes=50 * 1024 * 1024
        ),
    )(*(
        pltpu.with_memory_space_constraint(value, pltpu.HBM)
        for value in (
            terminal, jump, tangent,
            base_velocity.reshape(1, -1), base_shear.reshape(1, -1),
            jnp.asarray(high), jnp.asarray(low),
        )
    ))


def solution(mesh):
    sizes = tuple(mesh.shape[name] for name in ("seg", "gx", "gz"))
    split = P("seg", None, "gx", "gz", None)
    return jax.shard_map(
        functools.partial(shards, sizes),
        mesh=mesh,
        in_specs=(split, split, split, P(), P()),
        out_specs=split,
        check_vma=False,
    )
```

```python
import functools

import jax
import jax.numpy as jnp
import ml_dtypes
import numpy as np
from jax import lax
from jax.experimental import pallas as pl
from jax.experimental.pallas import tpu as pltpu
from jax.sharding import PartitionSpec as P

TIME_STEP = 0.15
DIFFUSE = 0.1
WALL_COEF = 0.0002
EPSILON = 1e-06
NEWTON_TURNS = 100
MESH = pl.DeviceIdType.MESH

NCOMP = 3
CX = 64
CZ = 16
LANES = 128
HALO = 8
XB = 16
NXO = CX + 2 * HALO
NXB = NXO + 4
ZIN = 40
ZBUF = 32
ZOUT = (32, 24, 24, 16)
CHUNK = 8
NCH = CX // CHUNK
AHEAD = 7
LAG = 3


def invert_newton(matrix):
    order = matrix.shape[0]
    identity = np.eye(order)
    scale_one = np.max(np.sum(np.abs(matrix), axis=0))
    scale_inf = np.max(np.sum(np.abs(matrix), axis=1))
    approx = matrix.T / (scale_one * scale_inf)
    for turn_index in range(NEWTON_TURNS):
        approx = approx @ (2.0 * identity - matrix @ approx)
    return approx


def wall_table(points):
    intervals = points - 1
    cheb_nodes = np.cos(np.pi * np.arange(points) / intervals)
    weights = np.ones(points)
    weights[0] = 2.0
    weights[-1] = 2.0
    weights = weights * (-1.0) ** np.arange(points)
    spread = cheb_nodes[:, None] - cheb_nodes[None, :]
    first_deriv = weights[:, None] / weights[None, :] / (spread + np.eye(points))
    first_deriv = first_deriv - np.eye(points) * first_deriv.sum(axis=1)[:, None]
    second = first_deriv @ first_deriv
    interior = np.eye(points - 2) - WALL_COEF * second[1:-1, 1:-1]
    helm_table = np.zeros((points, points))
    helm_table[1:-1, 1:-1] = invert_newton(interior)
    return helm_table.T.astype(np.float32)


def kernel(
    sizes,
    t_hbm, j_hbm, tan_hbm, vel_hbm, shear_hbm, hhi_hbm, hlo_hbm,
    out_hbm,
    tb, b0, w1, w2, w3, res, osend, orecv, oraw, ehi, elo, vel_ref, shear_ref, hhi_ref, hlo_ref, coef_ref, acc, ar_send, ar_recv_a, ar_mid, ar_recv_b,
    load_sem, const_sem, t_send, t_recv, zs_send, zs_recv, zt_send, zt_recv,
    ra_send, ra_recv, rb_send, rb_recv, o_send, o_recv, or_send, or_recv, out_sem,
):
    nseg, ngx, ngz = sizes
    seg, gx, gz = lax.axis_index("seg"), lax.axis_index("gx"), lax.axis_index("gz")
    nz = ngz // 2
    zc, core = gz // 2, lax.rem(gz, 2)
    before, after = lax.rem(seg + nseg - 1, nseg), lax.rem(seg + 1, nseg)
    zl, zr = lax.rem(gz + ngz - 1, ngz), lax.rem(gz + 1, ngz)
    ogx, ogz = 1 - gx, zc * 2 + (1 - core)
    left, right, partner = (seg, gx, zl), (seg, gx, zr), (seg, ogx, gz)
    group_a = [(seg, gx, ogz), (seg, ogx, gz), (seg, ogx, ogz)]
    group_b = [(seg, gx, lax.rem(zc + o, nz) * 2 + core) for o in range(1, nz)]
    outer = (seg, gx, lax.rem(gz + jnp.where(core == 0, ngz - 1, 1), ngz))

    def const_loads():
        return [
            pltpu.make_async_copy(src, dst, const_sem.at[i])
            for i, (src, dst) in enumerate((
                (vel_hbm, vel_ref), (shear_hbm, shear_ref), (hhi_hbm, hhi_ref), (hlo_hbm, hlo_ref),
            ))
        ]

    def block_loads(a, c):
        src = tan_hbm if a == 0 else j_hbm
        return [
            pltpu.make_async_copy(
                src.at[0, c, :, :, pl.ds(h * LANES, LANES)],
                b0.at[a * NCOMP + c, h, pl.ds(2 + HALO, CX), pl.ds(HALO, CZ), :],
                load_sem.at[(a * NCOMP + c) * 2 + h],
            )
            for h in range(2)
        ]

    later_loads = [(0, 1), (0, 2), (1, 0), (1, 1), (1, 2)]

    barrier = pltpu.get_barrier_semaphore()
    peers = [(before, gx, gz), (after, gx, gz), outer] + group_a + group_b
    for d in peers:
        pl.semaphore_signal(barrier, inc=1, device_id=d, device_id_type=MESH)
    for cp in block_loads(0, 0):
        cp.start()
    pl.semaphore_wait(barrier, len(peers))

    def t_copy(c, i):
        rows = pl.ds(i * CHUNK, CHUNK)
        return pltpu.make_async_remote_copy(
            src_ref=t_hbm.at[0, c, rows],
            dst_ref=tb.at[c, rows],
            send_sem=t_send.at[c * NCH + i],
            recv_sem=t_recv.at[c * NCH + i],
            device_id=(before, gx, gz),
            device_id_type=MESH,
        )

    for i in range(AHEAD):
        t_copy(i // NCH, i % NCH).start()
    for cp in const_loads():
        cp.start()
    for which in later_loads:
        for cp in block_loads(*which):
            cp.start()

    def strip(slot, x0, nx, side, send_sem, recv_sem):
        rows = pl.ds(2 + HALO + x0, nx)
        src = pl.ds(HALO, HALO) if side == 0 else pl.ds(HALO + CZ - HALO, HALO)
        dst = pl.ds(HALO + CZ, HALO) if side == 0 else pl.ds(0, HALO)
        return pltpu.make_async_remote_copy(
            src_ref=b0.at[slot, :, rows, src, :],
            dst_ref=b0.at[slot, :, rows, dst, :],
            send_sem=send_sem,
            recv_sem=recv_sem,
            device_id=left if side == 0 else right,
            device_id_type=MESH,
        )

    def tan_strip(c, side):
        k = c * 2 + side
        return strip(c, 0, CX, side, zs_send.at[k], zs_recv.at[k])

    def start_strip(c, i, side):
        k = (c * NCH + i) * 2 + side
        return strip(NCOMP + c, i * CHUNK, CHUNK, side, zt_send.at[k], zt_recv.at[k])

    for cp in block_loads(0, 0):
        cp.wait()
    for side in range(2):
        tan_strip(0, side).start()

    def zero_pads(s, _):
        for h in range(2):
            for lo, hi in ((0, 2 + HALO), (2 + HALO + CX, NXB)):
                b0[s, h, lo:hi, :, :] = jnp.zeros((hi - lo, ZIN, LANES), jnp.float32)
            b0[s, h, 2 + HALO:2 + HALO + CX, 2 * HALO + CZ:, :] = jnp.zeros(
                (CX, ZIN - 2 * HALO - CZ, LANES), jnp.float32)
        return 0

    lax.fori_loop(0, 2 * NCOMP, zero_pads, 0)
    for w in (w1, w2, w3):
        for s in range(2):
            for h in range(2):
                for lo in (0, NXB - 2):
                    w[s, h, lo:lo + 2, :, :] = jnp.zeros((2, ZBUF, LANES), jnp.float32)
                w[s, h, 2:NXB - 2, 24:, :] = jnp.zeros((NXB - 4, 8, LANES), jnp.float32)
    acc[...] = jnp.zeros_like(acc)
    for cp in const_loads():
        cp.wait()
    for which in later_loads:
        for cp in block_loads(*which):
            cp.wait()
    near, far = DIFFUSE * 16.0 / 12.0, DIFFUSE / 12.0
    push = TIME_STEP * vel_ref[...]
    coef_ref[0:1, :] = push * (8.0 / 12.0) + near
    coef_ref[1:2, :] = push * (-8.0 / 12.0) + near
    coef_ref[2:3, :] = push * (-1.0 / 12.0) - far
    coef_ref[3:4, :] = push * (1.0 / 12.0) - far
    coef_ref[4:5, :] = -TIME_STEP * shear_ref[...]

    def dot_rows(first, second):
        prod = first * second
        return jnp.sum(prod.reshape(-1, 8, LANES), axis=0)

    def square(i, _):
        c, x = i // NCH, lax.rem(i, NCH) * CHUNK
        for h in range(2):
            tau = b0[c, h, pl.ds(2 + HALO + x, CHUNK), HALO:HALO + CZ, :]
            acc[1] += dot_rows(tau, tau)
        return 0

    lax.fori_loop(0, NCOMP * NCH, square, 0)

    def piece(j):
        c, i = j // NCH, lax.rem(j, NCH)
        t_copy(c, i).wait_recv()
        rows = pl.ds(2 + HALO + i * CHUNK, CHUNK)
        for h in range(2):
            started = b0[NCOMP + c, h, rows, HALO:HALO + CZ, :] + tb[
                c, pl.ds(i * CHUNK, CHUNK), :, h * LANES:(h + 1) * LANES]
            b0[NCOMP + c, h, rows, HALO:HALO + CZ, :] = started
            acc[0] += dot_rows(started, b0[c, h, rows, HALO:HALO + CZ, :])
        start_strip(c, i, 0).start()
        start_strip(c, i, 1).start()

    def reduce_a(o):
        return pltpu.make_async_remote_copy(
            src_ref=ar_send, dst_ref=ar_recv_a.at[o], send_sem=ra_send.at[o], recv_sem=ra_recv.at[o],
            device_id=group_a[o], device_id_type=MESH)

    def reduce_b(o):
        return pltpu.make_async_remote_copy(
            src_ref=ar_mid, dst_ref=ar_recv_b.at[o], send_sem=rb_send.at[o], recv_sem=rb_recv.at[o],
            device_id=group_b[o], device_id_type=MESH)

    def outflow(c):
        sides = pl.ds(1, 1) if c == 0 else pl.ds(0, 2)
        return pltpu.make_async_remote_copy(
            src_ref=osend.at[c, sides], dst_ref=orecv.at[c, sides],
            send_sem=o_send.at[c], recv_sem=o_recv.at[c],
            device_id=partner, device_id_type=MESH)

    def raw_outflow(a):
        return pltpu.make_async_remote_copy(
            src_ref=res.at[a, 0, pl.ds(HALO + CX, HALO)], dst_ref=oraw.at[a],
            send_sem=or_send.at[a], recv_sem=or_recv.at[a],
            device_id=partner, device_id_type=MESH)

    def reduce_all():
        row = lax.broadcasted_iota(jnp.int32, (8, LANES), 0)
        top = jnp.sum(acc[0], axis=0, keepdims=True)
        low = jnp.sum(acc[1], axis=0, keepdims=True)
        ar_send[...] = jnp.where(row == 0, top, jnp.where(row == 1, low, 0.0))
        for o in range(3):
            reduce_a(o).start()
        for d in range(2):
            raw_outflow(d).start()
        for o in range(3):
            reduce_a(o).wait_recv()
        ar_mid[...] = ar_send[...] + ar_recv_a[0] + (ar_recv_a[1] + ar_recv_a[2])
        for o in range(nz - 1):
            reduce_b(o).start()
        for o in range(nz - 1):
            reduce_b(o).wait_recv()
        total = ar_mid[...]
        for o in range(nz - 1):
            total += ar_recv_b[o]
        sums = jnp.sum(total, axis=1, keepdims=True)
        acc[0] = jnp.broadcast_to(sums[0:1] / (sums[1:2] + EPSILON), (8, LANES))

    def send_outflow(c):
        along = acc[0, 0:1, 0:1]

        for side, at in ((0, HALO + CX), (1, 0)):
            if c > 0 or side > 0:
                osend[c, side] = res[1, c, at:at + HALO] - along * res[0, c, at:at + HALO]
        outflow(c).start()

    bufs = (b0, w1, w2, w3)

    def advance(k, n, a, c, first, count, sheared):
        half_set = jnp.minimum(c, 1)
        z = ZOUT[k]
        m = count * z
        src = bufs[k]
        slot = n if k == 0 else half_set
        slot0 = a * NCOMP if k == 0 else 0
        for h in range(2):
            cols = slice(h * LANES, (h + 1) * LANES)
            cs = [coef_ref[r:r + 1, cols] for r in range(5)]
            rows = {}

            def row(i):
                if i not in rows:
                    rows[i] = src[slot, h, first + i, 2:2 + z, :]
                return rows[i]

            for p in range(count // 2):
                both = []
                for i in (2 * p, 2 * p + 1):

                    def at(dz):
                        return src[slot, h, first + i + 2, 2 + dz:2 + dz + z, :]

                    e = 0.5 * row(i + 2)
                    e += (DIFFUSE * 16.0 / 12.0) * (at(1) + at(-1))
                    e += (-DIFFUSE / 12.0) * (at(2) + at(-2))
                    e += cs[0] * row(i + 3) + cs[1] * row(i + 1)
                    e += cs[2] * row(i + 4) + cs[3] * row(i)
                    if sheared:
                        e += cs[4] * src[slot0, h, first + i + 2, 2:2 + z, :]
                    both.append(e)
                e = jnp.concatenate(both, axis=0)
                hi = e.astype(jnp.bfloat16)
                ehi[2 * p * z:2 * (p + 1) * z, cols] = hi
                elo[2 * p * z:2 * (p + 1) * z, cols] = (e - hi.astype(jnp.float32)).astype(jnp.bfloat16)
        high = ehi[:m]
        out = jnp.dot(
            jnp.concatenate([high, elo[:m], high], axis=1),
            jnp.concatenate([hhi_ref[...], hhi_ref[...], hlo_ref[...]], axis=0),
            preferred_element_type=jnp.float32,
        )
        if k < 3:
            for h in range(2):
                bufs[k + 1][half_set, h, pl.ds(2 + first, count), 0:z, :] = out[
                    :, h * LANES:(h + 1) * LANES].reshape(count, z, LANES)
        else:
            res[a, c, pl.ds(first, count)] = out.reshape(count, z, 2 * LANES)

    def steps(n, a, c, sheared):
        for k in range(4):
            def block(b, _):
                advance(k, n, a, c, b * XB, XB, sheared)
                return 0

            lax.fori_loop(0, NXO // XB, block, 0)
            sent = n * 4 + k

            @pl.when(sent < NCOMP * NCH - AHEAD)
            def _():
                later = sent + AHEAD
                t_copy(later // NCH, lax.rem(later, NCH)).start()

            early = (sent >= 16) & (sent < 16 + LAG)

            @pl.when((sent >= LAG) & jnp.logical_not(early) & (n < 2 * NCOMP - 1))
            def _():
                piece(sent - LAG)

    def item(n, _):
        a, c = n // NCOMP, lax.rem(n, NCOMP)

        @pl.when(a == 0)
        def _():
            for side in range(2):
                tan_strip(c, side).wait_recv()

        @pl.when(n < NCOMP - 1)
        def _():
            for side in range(2):
                tan_strip(n + 1, side).start()

        @pl.when(n == 2 * NCOMP - 2)
        def _():
            for j in range(NCH * 2 - LAG, NCH * 2):
                piece(jnp.int32(j))

        @pl.when(n == 2 * NCOMP - 1)
        def _():
            def last(j, _):
                piece(j)
                return 0

            lax.fori_loop(20 - LAG, NCOMP * NCH, last, 0)
            reduce_all()
            for d in range(NCOMP - 1):
                send_outflow(d)

        @pl.when(a == 1)
        def _():
            def strips(i, _):
                start_strip(c, i, 0).wait_recv()
                start_strip(c, i, 1).wait_recv()
                return 0

            lax.fori_loop(0, NCH, strips, 0)

        @pl.when(n == 2 * NCOMP - 1)
        def _():
            for k in range(4):
                def edge(e, _):
                    advance(k, n, a, c, HALO - 2 * (k + 1) + e * (CX + 4 * (k + 1) - HALO), HALO, False)
                    return 0

                lax.fori_loop(0, 2, edge, 0)
            send_outflow(NCOMP - 1)

        @pl.when(c == 1)
        def _():
            steps(n, a, c, True)

        @pl.when(c != 1)
        def _():
            steps(n, a, c, False)
        return 0

    lax.fori_loop(0, 2 * NCOMP, item, 0)
    along = acc[0, 0:1, 0:1]

    def write(c, lo, n, k):
        return pltpu.make_async_copy(
            tb.at[c, pl.ds(lo, n)], out_hbm.at[0, c, pl.ds(lo, n)], out_sem.at[c * 3 + k])

    inner = CX - 2 * HALO
    for c in range(NCOMP):
        def mix(i, _):
            rows = pl.ds(2 * HALO + i * HALO, HALO)
            tb[c, pl.ds(HALO + i * HALO, HALO)] = res[1, c, rows] - along * res[0, c, rows]
            return 0

        lax.fori_loop(0, inner // HALO, mix, 0)
        write(c, HALO, inner, 0).start()
    for d in range(2):
        raw_outflow(d).wait_recv()
    for c in range(NCOMP):
        outflow(c).wait_recv()
        for side, at in ((0, 0), (1, CX - HALO)):
            own = res[1, c, HALO + at:2 * HALO + at] - along * res[0, c, HALO + at:2 * HALO + at]
            if c == 0 and side == 0:
                other = oraw[1] - along * oraw[0]
            else:
                other = orecv[c, side]
            tb[c, at:at + HALO] = own + other
        write(c, 0, HALO, 1).start()
        write(c, CX - HALO, HALO, 2).start()

    for c in range(NCOMP):
        write(c, HALO, inner, 0).wait()
        write(c, 0, HALO, 1).wait()
        write(c, CX - HALO, HALO, 2).wait()
        outflow(c).wait_send()
        for side in range(2):
            tan_strip(c, side).wait_send()

        @pl.loop(0, NCH)
        def _(i):
            t_copy(c, i).wait_send()
            start_strip(c, i, 0).wait_send()
            start_strip(c, i, 1).wait_send()
    for d in range(2):
        raw_outflow(d).wait_send()
    for o in range(3):
        reduce_a(o).wait_send()
    for o in range(nz - 1):
        reduce_b(o).wait_send()


def shards(sizes, terminal, jump, tangent, base_velocity, base_shear):
    table = wall_table(base_velocity.shape[0])
    high = table.astype(ml_dtypes.bfloat16)
    low = (table - high.astype(np.float32)).astype(ml_dtypes.bfloat16)
    nz = sizes[2] // 2
    f32 = jnp.float32
    dma = pltpu.SemaphoreType.DMA
    hbm = pl.BlockSpec(memory_space=pltpu.HBM)
    lanes2 = 2 * LANES
    return pl.pallas_call(
        functools.partial(kernel, sizes),
        out_shape=jax.ShapeDtypeStruct(terminal.shape, f32),
        in_specs=[hbm] * 7,
        out_specs=pl.BlockSpec(memory_space=pl.ANY),
        scratch_shapes=[
            pltpu.VMEM((NCOMP, CX, CZ, lanes2), f32),
            pltpu.VMEM((2 * NCOMP, 2, NXB, ZIN, LANES), f32),
            pltpu.VMEM((2, 2, NXB, ZBUF, LANES), f32),
            pltpu.VMEM((2, 2, NXB, ZBUF, LANES), f32),
            pltpu.VMEM((2, 2, NXB, ZBUF, LANES), f32),
            pltpu.VMEM((2, NCOMP, NXO, CZ, lanes2), f32),
            pltpu.VMEM((NCOMP, 2, HALO, CZ, lanes2), f32),
            pltpu.VMEM((NCOMP, 2, HALO, CZ, lanes2), f32),
            pltpu.VMEM((2, HALO, CZ, lanes2), f32),
            pltpu.VMEM((XB * ZBUF, lanes2), jnp.bfloat16),
            pltpu.VMEM((XB * ZBUF, lanes2), jnp.bfloat16),
            pltpu.VMEM((1, lanes2), f32),
            pltpu.VMEM((1, lanes2), f32),
            pltpu.VMEM((lanes2, lanes2), jnp.bfloat16),
            pltpu.VMEM((lanes2, lanes2), jnp.bfloat16),
            pltpu.VMEM((8, lanes2), f32),
            pltpu.VMEM((2, 8, LANES), f32),
            pltpu.VMEM((8, LANES), f32),
            pltpu.VMEM((3, 8, LANES), f32),
            pltpu.VMEM((8, LANES), f32),
            pltpu.VMEM((nz - 1, 8, LANES), f32),
            dma((4 * NCOMP,)),
            dma((4,)),
            dma((NCOMP * NCH,)),
            dma((NCOMP * NCH,)),
            dma((NCOMP * 2,)),
            dma((NCOMP * 2,)),
            dma((NCOMP * NCH * 2,)),
            dma((NCOMP * NCH * 2,)),
            dma((3,)),
            dma((3,)),
            dma((nz - 1,)),
            dma((nz - 1,)),
            dma((NCOMP,)),
            dma((NCOMP,)),
            dma((2,)),
            dma((2,)),
            dma((3 * NCOMP,)),
        ],
        compiler_params=pltpu.CompilerParams(
            collective_id=0, has_side_effects=True, vmem_limit_bytes=50 * 1024 * 1024
        ),
    )(*(
        pltpu.with_memory_space_constraint(value, pltpu.HBM)
        for value in (
            terminal, jump, tangent,
            base_velocity.reshape(1, -1), base_shear.reshape(1, -1),
            jnp.asarray(high), jnp.asarray(low),
        )
    ))


def solution(mesh):
    sizes = tuple(mesh.shape[name] for name in ("seg", "gx", "gz"))
    split = P("seg", None, "gx", "gz", None)
    return jax.shard_map(
        functools.partial(shards, sizes),
        mesh=mesh,
        in_specs=(split, split, split, P(), P()),
        out_specs=split,
        check_vma=False,
    )
```
